128 devices in a mesh: gx: 32 (over z, y, core), gy: 4 (over x).
Axes of the slice: x: 4, y: 4, z: 4, core: 2. Of those that a mesh axis runs over, the one named last changes fastest.
Arguments:
- scalar: float32 [2, 512, 32, 4, 128], P(None, None, 'gx', 'gy'), may hold values from -6 to 6
- velocity: float32 [3, 2, 512, 32, 4, 128], P(None, None, None, 'gx', 'gy'), may hold values from -1 to 1
- diffusivity: float32 [2, 32, 4, 128], P(None, 'gx', 'gy'), may hold values from 0.005 to 0.05
- recv_owner: int32 [262144, 1], P(('gx', 'gy')), may hold values from 0 to 127; in each aligned block of 2048 rows (0 to 2047, 2048 to 4095, ...) at most 32 rows name the same one
- donor_elem: int32 [262144], P(('gx', 'gy')), may hold values from 0 to 127
- recv_point: int32 [262144], P(('gx', 'gy')), may hold values from 0 to 65535
- recv_coords: float32 [3, 262144], P(None, ('gx', 'gy')), may hold values from -1 to 1
Outputs:
- advanced: float32 [2, 512, 32, 4, 128], P(None, None, 'gx', 'gy')
The draws below stay inside these ranges and needn't reach their ends.
Inputs may be any that keep to these rules, and one draw needn't show every extreme that they name: `recv_owner`: among the 2048 receivers of one device no owner is named more than 32 times, a bound that some block reaches.
All inputs are finite; a program needn't handle non-finite values.
Results may differ from the reference program's by a relative error of at most 0.0003.
Values sent between devices are 32-bit elements; how exact they have to be, the bound alone decides.
No kernel may reach another device: no remote copies, remote signals or barrier semaphores. Data moves between devices by JAX's collectives and lax.ppermute only.
A program may use at most 128 MiB of HBM per device.

```python
import math
import jax
import jax.numpy as jnp
import numpy as np
from jax import lax

KX = 1
KY = 1
EZ = 128
R_DEV = 2048
ELEMS = 128
CAP = 32
EX = 32
EY = 4
RECV = 262144
N_GY = 4
DEVICES = 128


def set_ends(entries, own_key, smallest, largest):
    spot = [jax.random.randint(jax.random.fold_in(own_key, axis), (), 0, length) for axis, length in enumerate(entries.shape)]
    main_axis = entries.shape.index(max(entries.shape))
    next_to = spot[:main_axis] + [(spot[main_axis] + 1) % entries.shape[main_axis]] + spot[main_axis + 1:]
    return entries.at[tuple(spot)].set(smallest).at[tuple(next_to)].set(largest)


def block_levels(own_key, extent, shards, smallest, top_value):
    def one(dim, parts):
        heights = jax.random.uniform(jax.random.fold_in(jax.random.fold_in(own_key, 6), dim), (parts,), jnp.float32, smallest / len(shards), top_value / len(shards))
        return jnp.repeat(jnp.exp(heights), extent[dim] // parts).reshape((-1,) + (1,) * (len(extent) - dim - 1))

    factor_of = one(*shards[0])
    for cut in shards[1:]:
        factor_of = factor_of * one(*cut)
    return factor_of


def routed_block(key, own, number, rows, amount, top, most, skew):
    order = jax.random.permutation(key, amount)
    crowded, usual = load_shares(amount, rows * top, most, skew, True), load_shares(amount, rows * top, most, skew, False)
    places = jnp.arange(amount)

    def named(sizes, offset_by):
        used = int((sizes > 0).sum())
        fixed = max(1, used // 4)
        passed = fixed + (places - fixed + offset_by * (used - fixed)) % max(1, amount - fixed)
        return jnp.zeros((amount,), jnp.int32).at[order[jnp.where(places < fixed, places, passed)]].set(jnp.asarray(sizes, jnp.int32))

    sizes = jnp.where(number % 4 == 0, named(crowded, number // 4), named(usual, number - number // 4 - 1))
    mixed = jax.random.permutation(jax.random.fold_in(own, 3), amount)
    source_of, sink = mixed[0:amount // 2 * 2:2], mixed[1:amount // 2 * 2:2]
    slack = jnp.minimum(sizes[source_of] - 1, most - sizes[sink]) // 2
    slack = jnp.where((source_of == order[0]) | (sink == order[0]) | (sizes[sink] == 0), 0, jnp.maximum(slack, 0))
    passed = jax.random.randint(jax.random.fold_in(own, 4), (amount // 2,), 0, 1 << 20) % (slack + 1)
    sizes = sizes.at[source_of].add(-passed).at[sink].add(passed)
    members = jnp.searchsorted(jnp.cumsum(sizes), jnp.arange(rows * top), side="right").astype(jnp.int32)
    grid = members.reshape(top, rows).T
    grid = grid[jax.random.permutation(jax.random.fold_in(own, 1), rows)]
    offset_by = jax.random.randint(jax.random.fold_in(own, 2), (rows, 1), 0, top)
    return jnp.take_along_axis(grid, (jnp.arange(top)[None, :] + offset_by) % top, axis=1)


def load_shares(number_of, total, reach, lean, full):
    portions = [(1 << 20) // math.isqrt(grade ** lean) + 1 for grade in range(1, number_of + 1)]
    largest = reach if full else min(reach, max(-(-total // number_of), total * portions[0] // sum(portions)))
    least = 1 if total - largest >= number_of - 1 else 0
    holding, rest = [largest] + [least] * (number_of - 1), total - largest - least * (number_of - 1)
    while rest > 0:
        movable = [i for i in range(1, number_of) if holding[i] < largest] or [i for i in range(1, number_of) if holding[i] < reach]
        pool, remaining = sum([portions[i] for i in movable]), rest
        for i in movable:
            addition = min(reach - holding[i], max(1, remaining * portions[i] // pool), rest)
            holding[i] = holding[i] + addition
            rest = rest - addition
    return np.array(holding)


def bell_draw(rng, extent, scale, bound, shards=(), kind=jnp.bfloat16):
    loudness = block_levels(rng, extent, shards, -0.22, 0.18) if shards else 1.0
    result = jax.random.normal(rng, extent, jnp.float32) * scale * loudness
    return jnp.minimum(jnp.maximum(result, -bound), bound).astype(kind)


def setup_inputs(seed: int = 0) -> dict:
    streams_of = jax.random.split(jax.random.key(seed), 8)
    scalar = bell_draw(streams_of[0], (2, 512, EX, EY, EZ), 1.0, 6.0, ((2, 32), (3, 4)), jnp.float32)
    velocity = jnp.clip(jax.random.uniform(streams_of[1], (3, 2, 512, EX, EY, EZ), jnp.float32, -1.0, 1.0) * block_levels(streams_of[1], (3, 2, 512, EX, EY, EZ), ((3, 32), (4, 4)), -0.4, 0.0), -1.0, 1.0)
    diffusivity = jnp.clip(jnp.exp(math.log(0.05) - 2.3025851 * jax.random.uniform(streams_of[2], (2, EX, EY, EZ), jnp.float32) ** block_levels(streams_of[2], (2, EX, EY, EZ), ((1, 32), (2, 4)), -0.2, 0.2)), 0.005, 0.05)
    recv_owner_keys = jax.random.split(jax.random.fold_in(streams_of[3], 1), RECV // R_DEV)
    recv_owner_turns = jax.random.permutation(jax.random.fold_in(streams_of[3], 3), RECV // R_DEV)
    recv_owner = jax.vmap(lambda own, number: routed_block(jax.random.fold_in(streams_of[3], 2), own, number, R_DEV, DEVICES, 1, CAP, 2))(recv_owner_keys, recv_owner_turns).reshape((RECV, 1))
    donor_elem = set_ends(jax.random.randint(streams_of[4], (RECV,), 0, ELEMS), jax.random.fold_in(streams_of[4], 1), 0, ELEMS - 1).astype(jnp.int32)
    recv_point = set_ends(jax.random.randint(streams_of[5], (RECV,), 0, 512 * ELEMS), jax.random.fold_in(streams_of[5], 1), 0, (512 * ELEMS) - 1).astype(jnp.int32)
    recv_coords = jnp.clip(jax.random.uniform(streams_of[6], (3, RECV), jnp.float32, -1.0, 1.0) * block_levels(streams_of[6], (3, RECV), ((1, 128),), -0.4, 0.0), -1.0, 1.0)
    return {"scalar": scalar, "velocity": velocity, "diffusivity": diffusivity, "recv_owner": recv_owner, "donor_elem": donor_elem, "recv_point": recv_point, "recv_coords": recv_coords}


time_step = 0.01
penalty_rate = 50.0
metric = 2.0
volume_factor = 0.125
node_inner = [0.871740148509606615337, 0.591700181433142302144, 0.209299217902478868769]


def legendre_seven(point):
    before, current = 1.0, point
    for order in range(1, 7):
        before, current = current, ((2 * order + 1) * point * current - order * before) / (order + 1)
    return current


def gll_tables():
    degree = 7
    gll_nodes = [-1.0, -node_inner[0], -node_inner[1], -node_inner[2], node_inner[2], node_inner[1], node_inner[0], 1.0]
    end_values = [legendre_seven(v) for v in gll_nodes]
    weights = [2.0 / (degree * (degree + 1) * v * v) for v in end_values]
    derivative = [[0.0] * 8 for _ in range(8)]
    for a in range(8):
        for b in range(8):
            if a != b:
                derivative[a][b] = end_values[a] / (end_values[b] * (gll_nodes[a] - gll_nodes[b]))
    derivative[0][0] = -degree * (degree + 1) / 4.0
    derivative[7][7] = degree * (degree + 1) / 4.0
    weight_row = jnp.asarray(weights, jnp.float32)
    cube_weights = weight_row[:, None, None] * weight_row[None, :, None] * weight_row[None, None, :]
    return gll_nodes, cube_weights, derivative


def lagrange_rows(position, gll_nodes):
    columns = []
    for j in range(8):
        factor = jnp.ones_like(position)
        for m in range(8):
            if m != j:
                factor = factor * ((position - gll_nodes[m]) / (gll_nodes[j] - gll_nodes[m]))
        columns.append(factor)
    return jnp.stack(columns, axis=-1)


def element_rate(values, velocity, diffusivity, derivative, cube_weights):
    highest = lax.Precision.HIGHEST
    grad_x = metric * jnp.einsum('ai,ijkxyz->ajkxyz', derivative, values, precision=highest)
    grad_y = metric * jnp.einsum('bj,ijkxyz->ibkxyz', derivative, values, precision=highest)
    grad_z = metric * jnp.einsum('ck,ijkxyz->ijcxyz', derivative, values, precision=highest)
    mass_local = volume_factor * cube_weights[:, :, :, None, None, None]
    advect = velocity[0] * grad_x + velocity[1] * grad_y + velocity[2] * grad_z
    scaled = (metric * mass_local) * diffusivity[None, None, None]
    diffuse = jnp.einsum('ai,ajkxyz->ijkxyz', derivative, scaled * grad_x, precision=highest)
    diffuse = diffuse + jnp.einsum('bj,ibkxyz->ijkxyz', derivative, scaled * grad_y, precision=highest)
    diffuse = diffuse + jnp.einsum('ck,ijcxyz->ijkxyz', derivative, scaled * grad_z, precision=highest)
    return -(mass_local * advect) - diffuse


def face_sum(values, pdim, edim, next_slab, prev_slab):
    left = lax.index_in_dim(values, 0, pdim, keepdims=True)
    right = lax.index_in_dim(values, 7, pdim, keepdims=True)
    count = values.shape[edim]
    after = jnp.concatenate([lax.slice_in_dim(left, 1, count, axis=edim), next_slab], axis=edim)
    before = jnp.concatenate([prev_slab, lax.slice_in_dim(right, 0, count - 1, axis=edim)], axis=edim)
    middle = lax.slice_in_dim(values, 1, 7, axis=pdim)
    return jnp.concatenate([left + before, middle, right + after], axis=pdim)


def assemble(values):
    for pdim, edim in ((1, 4), (2, 5), (3, 6)):
        slab = lax.index_in_dim(lax.index_in_dim(values, 0, pdim, keepdims=True), 0, edim, keepdims=True)
        zeros_slab = jnp.zeros_like(slab)
        values = face_sum(values, pdim, edim, zeros_slab, zeros_slab)
    return values


def reference(scalar, velocity, diffusivity, recv_owner, donor_elem, recv_point, recv_coords):
    gll_nodes, cube_np, derivative_np = gll_tables()
    derivative = jnp.asarray(derivative_np, jnp.float32)
    cube_weights = jnp.asarray(cube_np, jnp.float32)
    cube_flat = cube_weights.reshape(512)
    shape_full = (2, 8, 8, 8, EX, EY, EZ)
    elems = KX * KY * EZ
    flow = velocity.reshape((3,) + shape_full)
    mass_total = assemble(jnp.broadcast_to(volume_factor * cube_weights[None, :, :, :, None, None, None], shape_full))

    rows = jnp.arange(RECV, dtype=jnp.int32)
    device = rows // R_DEV
    local_row = rows % R_DEV
    dev_x = device // N_GY
    dev_y = device % N_GY
    own_mesh = (local_row >= R_DEV // 2).astype(jnp.int32)
    donor_mesh = 1 - own_mesh
    owners = recv_owner[:, 0]
    donor_x = (owners // N_GY) * KX + donor_elem // (KY * EZ)
    donor_y = (owners % N_GY) * KY + (donor_elem // EZ) % KY
    donor_z = donor_elem % EZ
    point_q = recv_point // elems
    point_e = recv_point % elems
    recv_x = dev_x * KX + point_e // (KY * EZ)
    recv_y = dev_y * KY + (point_e // EZ) % KY
    recv_z = point_e % EZ
    flat_index = ((own_mesh * 512 + point_q) * EX + recv_x) * (EY * EZ) + recv_y * EZ + recv_z
    basis_x = lagrange_rows(recv_coords[0], gll_nodes)
    basis_y = lagrange_rows(recv_coords[1], gll_nodes)
    basis_z = lagrange_rows(recv_coords[2], gll_nodes)
    point_mass = volume_factor * cube_flat[point_q]

    def blocks(array):
        return array.reshape((DEVICES, R_DEV) + array.shape[1:])

    def interpolate(values_five):
        def one_block(pieces):
            mesh_ids, elem_x, elem_y, elem_z, wx, wy, wz = pieces
            element_values = values_five[mesh_ids, :, elem_x, elem_y, elem_z]
            tensor_weights = (wx[:, :, None, None] * wy[:, None, :, None] * wz[:, None, None, :]).reshape(-1, 512)
            return jnp.sum(element_values * tensor_weights, axis=1)
        pieces = (blocks(donor_mesh), blocks(donor_x), blocks(donor_y), blocks(donor_z),
                  blocks(basis_x), blocks(basis_y), blocks(basis_z))
        return lax.map(one_block, pieces).reshape(RECV)

    def rate(values):
        local = jnp.stack([element_rate(values[m], flow[:, m], diffusivity[m], derivative, cube_weights) for m in range(2)])
        donor_values = interpolate(values.reshape(2, 512, EX, EY, EZ))
        current = values.reshape(-1)[flat_index]
        added = penalty_rate * point_mass * (donor_values - current)
        local = local.reshape(-1).at[flat_index].add(added).reshape(shape_full)
        return assemble(local) / mass_total

    start = scalar.reshape(shape_full)
    first = start + time_step * rate(start)
    second = 0.75 * start + 0.25 * (first + time_step * rate(first))
    third = start / 3.0 + (2.0 / 3.0) * (second + time_step * rate(second))
    return third.reshape(2, 512, EX, EY, EZ)
```

```python
import jax
import jax.numpy as jnp
import numpy as np
from jax import lax
from jax.experimental import pallas as pl
from jax.experimental.pallas import tpu as pltpu
from jax.sharding import PartitionSpec as P

time_step = 0.01
penalty_rate = 50.0
metric = 2.0
volume_factor = 0.125
node_inner = [0.8717401485096066, 0.5917001814331423, 0.20929921790247888]
f32 = jnp.float32
bf16 = jnp.bfloat16
i32 = jnp.int32


def legendre_seven(point):
    before, current = (1.0, point)
    for order in range(1, 7):
        before, current = (
            current,
            ((2 * order + 1) * point * current - order * before) / (order + 1),
        )
    return current


def gll_tables():
    degree = 7
    gll_nodes = [-1.0] + [-v for v in node_inner] + node_inner[::-1] + [1.0]
    end_values = [legendre_seven(v) for v in gll_nodes]
    weights = [2.0 / (degree * (degree + 1) * v * v) for v in end_values]
    derivative = [[0.0] * 8 for _ in range(8)]
    for a in range(8):
        for b in range(8):
            if a != b:
                derivative[a][b] = end_values[a] / (end_values[b] * (gll_nodes[a] - gll_nodes[b]))
    derivative[0][0] = -degree * (degree + 1) / 4.0
    derivative[7][7] = degree * (degree + 1) / 4.0
    return (gll_nodes, weights, derivative)


NODES, WEIGHTS, DERIV = gll_tables()
DERIV_T = [[DERIV[b][a] for b in range(8)] for a in range(8)]


def split_two(x):
    hi = x.astype(bf16)
    lo = (x - hi.astype(f32)).astype(bf16)
    return hi, lo


def block_matrix(table):
    full = np.kron(np.eye(16), np.asarray(table, np.float64)).astype(np.float32)
    hi = full.astype(jnp.bfloat16)
    lo = (full - hi.astype(np.float32)).astype(jnp.bfloat16)
    return np.concatenate([hi, lo, hi], axis=1)


def apply_table(table, pieces):
    even = [pieces[b] + pieces[7 - b] for b in range(4)]
    odd = [pieces[b] - pieces[7 - b] for b in range(4)]
    outs = [None] * 8
    for a in range(4):
        s = None
        d = None
        for b in range(4):
            cs = 0.5 * (table[a][b] - table[a][7 - b])
            cd = 0.5 * (table[a][b] + table[a][7 - b])
            s = cs * odd[b] if s is None else s + cs * odd[b]
            d = cd * even[b] if d is None else d + cd * even[b]
        outs[a] = d + s
        outs[7 - a] = s - d
    return outs


def dot_nn(a, b):
    return lax.dot_general(a, b, (((1,), (0,)), ((), ())), preferred_element_type=f32)


def dot_nt(a, b):
    return lax.dot_general(a, b, (((1,), (1,)), ((), ())), preferred_element_type=f32)


def one_hot_rows(row, count, dtype=bf16):
    ids = lax.broadcasted_iota(i32, (count, row.shape[-1]), 0)
    return jnp.where(ids == row, 1.0, 0.0).astype(dtype)


def weight_rows():
    k = lax.broadcasted_iota(i32, (8, 128), 0)
    out = jnp.zeros((8, 128), f32)
    for j in range(8):
        out = jnp.where(k == j, WEIGHTS[j], out)
    return out


def query_kernel(owner_ref, donor_ref, coords_ref, payload_ref, rank_ref):
    rows = owner_ref.shape[1]
    half = rows // 2
    owner = owner_ref[...]
    step = 256
    before = (
        lax.broadcasted_iota(i32, (step, step), 0) < lax.broadcasted_iota(i32, (step, step), 1)
    )
    before = jnp.where(before, 1.0, 0.0).astype(bf16)
    total = jnp.zeros((128, 1), f32)
    acc = [jnp.zeros((128, 128), f32) for _ in range(3)]
    for c in range(rows // step):
        sl = slice(c * step, (c + 1) * step)
        oh = one_hot_rows(owner[:, sl], 128)
        ohf = oh.astype(f32)
        cum = dot_nn(oh, before) + total
        rank = jnp.sum(cum * ohf, axis=0, keepdims=True)
        total = total + jnp.sum(ohf, axis=1, keepdims=True)
        rank_i = rank.astype(i32)
        rank_ref[:, sl] = rank_i
        pick = lax.broadcasted_iota(i32, (32, step), 0) == rank_i
        col = lax.broadcasted_iota(i32, (1, step), 1) + c * step
        ident = (jnp.where(col < half, 128, 0) + donor_ref[:, sl]).astype(f32)
        parts = [[], [], []]
        for v in range(3):
            x = coords_ref[v : v + 1, sl]
            hi = x.astype(bf16).astype(f32)
            rest = x - hi
            mid = rest.astype(bf16).astype(f32)
            for p, val in enumerate((hi, mid, rest - mid)):
                parts[p].append(jnp.where(pick, val, 0.0).astype(bf16))
        zero = jnp.zeros((32, step), bf16)
        parts[0].append(jnp.where(pick, ident, 0.0).astype(bf16))
        parts[1].append(zero)
        parts[2].append(zero)
        for p in range(3):
            acc[p] = acc[p] + dot_nt(oh, jnp.concatenate(parts[p], axis=0))
    payload_ref[...] = acc[0] + (acc[1] + acc[2])


def prepare_kernel(flags_ref, point_ref, load_ref, inv_ref):
    half = point_ref.shape[1] // 2
    wk = weight_rows()
    for m in range(2):
        point = point_ref[:, m * half : (m + 1) * half]
        q = lax.shift_right_logical(point, 7)
        e = lax.bitwise_and(point, 127)
        count = dot_nt(one_hot_rows(q, 512), one_hot_rows(e, 128))
        for ij in range(64):
            c = penalty_rate * volume_factor * WEIGHTS[ij // 8] * WEIGHTS[ij % 8]
            load_ref[m, ij * 8 : ij * 8 + 8, :] = (c * wk) * count[ij * 8 : ij * 8 + 8, :]
    k = lax.broadcasted_iota(i32, (8, 128), 0)
    e = lax.broadcasted_iota(i32, (8, 128), 1)
    shared = ((k == 0) & (e > 0)) | ((k == 7) & (e < 127))
    base = time_step / (volume_factor * wk * jnp.where(shared, 2.0, 1.0))
    for ij in range(64):
        i, j = ij // 8, ij % 8
        val = base * (1.0 / (WEIGHTS[i] * WEIGHTS[j]))
        if i == 0:
            val = val * flags_ref[0]
        if i == 7:
            val = val * flags_ref[1]
        if j == 0:
            val = val * flags_ref[2]
        if j == 7:
            val = val * flags_ref[3]
        inv_ref[ij * 8 : ij * 8 + 8, :] = val


def local_kernel(u_ref, vel_ref, nu_ref, load_ref, dz_ref, dzt_ref, out_ref, ax_ref, ay_ref, fz_ref):
    wk = weight_rows()

    def depth(table, pick):
        chunks = []
        for c in range(4):
            rows = slice(c * 128, (c + 1) * 128)
            hi, lo = split_two(jnp.concatenate([pick(0, rows), pick(1, rows)], axis=1))
            chunks.append(dot_nn(table, jnp.concatenate([hi, hi, lo], axis=0)))
        return chunks

    az = depth(dz_ref[...], lambda m, rows: u_ref[m, rows, :])
    for m in range(2):
        for j in range(8):
            outs = apply_table(DERIV, [u_ref[m, i * 64 + j * 8 : i * 64 + j * 8 + 8, :] for i in range(8)])
            for i in range(8):
                ax_ref[m, i * 64 + j * 8 : i * 64 + j * 8 + 8, :] = outs[i]
        wnu = 4.0 * volume_factor * wk * nu_ref[m : m + 1, :]
        wad = 2.0 * volume_factor * wk
        for i in range(8):
            outs = apply_table(DERIV, [u_ref[m, i * 64 + j * 8 : i * 64 + j * 8 + 8, :] for j in range(8)])
            fluxes = []
            for j in range(8):
                ij = i * 8 + j
                rows = slice(ij * 8, ij * 8 + 8)
                c = WEIGHTS[i] * WEIGHTS[j]
                gx = ax_ref[m, rows, :]
                gy = outs[j]
                gz = az[ij // 16][(ij % 16) * 8 : (ij % 16) * 8 + 8, m * 128 : (m + 1) * 128]
                adv = vel_ref[0, m, rows, :] * gx + vel_ref[1, m, rows, :] * gy + vel_ref[2, m, rows, :] * gz
                out_ref[m, rows, :] = -((c * wad) * adv) - load_ref[m, rows, :] * u_ref[m, rows, :]
                flux = c * wnu
                ax_ref[m, rows, :] = flux * gx
                fz_ref[m, rows, :] = flux * gz
                fluxes.append(flux * gy)
            outs = apply_table(DERIV_T, fluxes)
            for j in range(8):
                rows = slice(i * 64 + j * 8, i * 64 + j * 8 + 8)
                out_ref[m, rows, :] = out_ref[m, rows, :] - outs[j]
    bz = depth(dzt_ref[...], lambda m, rows: fz_ref[m, rows, :])
    for m in range(2):
        for j in range(8):
            outs = apply_table(DERIV_T, [ax_ref[m, i * 64 + j * 8 : i * 64 + j * 8 + 8, :] for i in range(8)])
            for i in range(8):
                ij = i * 8 + j
                rows = slice(ij * 8, ij * 8 + 8)
                gz = bz[ij // 16][(ij % 16) * 8 : (ij % 16) * 8 + 8, m * 128 : (m + 1) * 128]
                out_ref[m, rows, :] = (out_ref[m, rows, :] - outs[i]) - gz


def interpolate(u, received_ref, ans_ref, wx_ref, wy_ref, wz_ref):
    parts = [split_two(v) for v in u]
    cat = jnp.concatenate([parts[0][0], parts[1][0], parts[0][1], parts[1][1]], axis=1)
    turned = received_ref[...].T
    for v, ref in enumerate((wx_ref, wy_ref, wz_ref)):
        x = turned[v * 32 : v * 32 + 32, :]
        diff = [x - NODES[m] for m in range(8)]
        pre = [None] * 8
        suf = [None] * 8
        for m in range(1, 8):
            pre[m] = diff[m - 1] if pre[m - 1] is None else pre[m - 1] * diff[m - 1]
        for m in range(6, -1, -1):
            suf[m] = diff[m + 1] if suf[m + 1] is None else suf[m + 1] * diff[m + 1]
        for j in range(8):
            c = 1.0
            for m in range(8):
                if m != j:
                    c = c / (NODES[j] - NODES[m])
            w = suf[j] if pre[j] is None else (pre[j] if suf[j] is None else pre[j] * suf[j])
            w = w * c
            if ref is wz_ref:
                ref[:, j, :] = w
            else:
                ref[j] = w
    ids = turned[96:128, :].astype(i32)
    rows = []
    for g in range(16):
        hot = [one_hot_rows(ids[s : s + 1, :], 256) for s in (2 * g, 2 * g + 1)]
        hot = jnp.concatenate(hot, axis=1)
        got = dot_nn(cat, jnp.concatenate([hot, hot], axis=0))
        for b in range(2):
            s = 2 * g + b
            total = None
            for j in range(8):
                acc = None
                for i in range(8):
                    term = wx_ref[i, s : s + 1, :] * got[i * 64 + j * 8 : i * 64 + j * 8 + 8, b * 128 : (b + 1) * 128]
                    acc = term if acc is None else acc + term
                acc = acc * wy_ref[j, s : s + 1, :]
                total = acc if total is None else total + acc
            rows.append(jnp.sum(total * wz_ref[s], axis=0, keepdims=True))
    answers = jnp.concatenate(rows + [jnp.zeros((96, 128), f32)], axis=0)
    ans_ref[...] = answers.T


def first_kernel(u_ref, received_ref, ans_ref, wx_ref, wy_ref, wz_ref):
    interpolate([u_ref[0], u_ref[1]], received_ref, ans_ref, wx_ref, wy_ref, wz_ref)


def penalty_kernel(replies_ref, owner_ref, rank_ref, point_ref, local_ref, out_ref, xl_ref, xr_ref, yl_ref, yr_ref):
    half = point_ref.shape[1] // 2
    hi, lo = split_two(replies_ref[...].T[0:32, :])
    lhs = jnp.concatenate([hi, lo], axis=1)
    wk = weight_rows()
    for m in range(2):
        sl = slice(m * half, (m + 1) * half)
        oh = one_hot_rows(owner_ref[:, sl], 128)
        got = dot_nn(lhs, jnp.concatenate([oh, oh], axis=0))
        pick = lax.broadcasted_iota(i32, (32, half), 0) == rank_ref[:, sl]
        g = jnp.sum(jnp.where(pick, got, 0.0), axis=0, keepdims=True)
        ghi = g.astype(bf16).astype(f32)
        glo = g - ghi
        point = point_ref[:, sl]
        q = lax.shift_right_logical(point, 7)
        e = lax.bitwise_and(point, 127)
        at = lax.broadcasted_iota(i32, (128, half), 0) == e
        rhs = jnp.concatenate(
            [jnp.where(at, ghi, 0.0).astype(bf16), jnp.where(at, glo, 0.0).astype(bf16)], axis=0
        )
        both = dot_nt(one_hot_rows(q, 512), rhs)
        summed = both[:, 0:128] + both[:, 128:256]
        for ij in range(64):
            rows = slice(ij * 8, ij * 8 + 8)
            i, j = ij // 8, ij % 8
            c = penalty_rate * volume_factor * WEIGHTS[i] * WEIGHTS[j]
            val = local_ref[m, rows, :] + (c * wk) * summed[rows, :]
            out_ref[m, rows, :] = val
            if i == 0:
                xl_ref[m, j * 8 : j * 8 + 8, :] = val
            if i == 7:
                xr_ref[m, j * 8 : j * 8 + 8, :] = val
            if j == 0:
                yl_ref[m, i * 8 : i * 8 + 8, :] = val
            if j == 7:
                yr_ref[m, i * 8 : i * 8 + 8, :] = val


def edge_kernel(yl_ref, yr_ref, xn_ref, xp_ref, yl_out, yr_out):
    for m in range(2):
        for src, dst, j in ((yl_ref, yl_out, 0), (yr_ref, yr_out, 7)):
            dst[m, 8:56, :] = src[m, 8:56, :]
            dst[m, 0:8, :] = src[m, 0:8, :] + xp_ref[m, j * 8 : j * 8 + 8, :]
            dst[m, 56:64, :] = src[m, 56:64, :] + xn_ref[m, j * 8 : j * 8 + 8, :]


def finish(blend, v_ref, xn_ref, xp_ref, yn_ref, yp_ref, inv_ref, start_ref, u_ref, new_ref, work_ref):
    lane = lax.broadcasted_iota(i32, (64, 128), 1)
    for m in range(2):
        for ij in range(64):
            rows = slice(ij * 8, ij * 8 + 8)
            i, j = ij // 8, ij % 8
            val = v_ref[m, rows, :]
            if j == 0:
                val = val + yp_ref[m, i * 8 : i * 8 + 8, :]
            elif j == 7:
                val = val + yn_ref[m, i * 8 : i * 8 + 8, :]
            if i == 0 and j not in (0, 7):
                val = val + xp_ref[m, j * 8 : j * 8 + 8, :]
            elif i == 7 and j not in (0, 7):
                val = val + xn_ref[m, j * 8 : j * 8 + 8, :]
            elif i == 0:
                val = val + xp_ref[m, j * 8 : j * 8 + 8, :]
            elif i == 7:
                val = val + xn_ref[m, j * 8 : j * 8 + 8, :]
            work_ref[m, rows, :] = val
        left = work_ref[m, pl.ds(0, 64, stride=8), :]
        right = work_ref[m, pl.ds(7, 64, stride=8), :]
        work_ref[m, pl.ds(0, 64, stride=8), :] = left + jnp.where(lane > 0, pltpu.roll(right, 1, 1), 0.0)
        work_ref[m, pl.ds(7, 64, stride=8), :] = right + jnp.where(lane < 127, pltpu.roll(left, 127, 1), 0.0)
        new = u_ref[m] + inv_ref[...] * work_ref[m]
        if blend is not None:
            new = blend[0] * start_ref[m] + blend[1] * new
        new_ref[m] = new


def step_kernel(blend, v_ref, xn_ref, xp_ref, yn_ref, yp_ref, inv_ref, start_ref, u_ref, received_ref,
                new_ref, ans_ref, work_ref, wx_ref, wy_ref, wz_ref):
    finish(blend, v_ref, xn_ref, xp_ref, yn_ref, yp_ref, inv_ref, start_ref, u_ref, new_ref, work_ref)
    interpolate([new_ref[0], new_ref[1]], received_ref, ans_ref, wx_ref, wy_ref, wz_ref)


def last_kernel(blend, v_ref, xn_ref, xp_ref, yn_ref, yp_ref, inv_ref, start_ref, u_ref, new_ref, work_ref):
    finish(blend, v_ref, xn_ref, xp_ref, yn_ref, yp_ref, inv_ref, start_ref, u_ref, new_ref, work_ref)


def call(kernel, outs, ins, scratch=(), smem_first=False):
    specs = [pl.BlockSpec(memory_space=pltpu.VMEM)] * len(ins)
    if smem_first:
        specs[0] = pl.BlockSpec(memory_space=pltpu.SMEM)
    return pl.pallas_call(
        kernel,
        out_shape=[jax.ShapeDtypeStruct(s, d) for s, d in outs],
        in_specs=specs,
        out_specs=[pl.BlockSpec(memory_space=pltpu.VMEM)] * len(outs),
        scratch_shapes=list(scratch),
        compiler_params=pltpu.CompilerParams(vmem_limit_bytes=24 << 20),
    )(*ins)


def passed_along(value, axis, steps):
    count = lax.axis_size(axis)
    leading, last = (max(0, -steps), min(count, count - steps))
    return lax.ppermute(value, axis, [(source, source + steps) for source in range(leading, last)])


def exchange(x):
    return lax.all_to_all(x, ("gx", "gy"), split_axis=0, concat_axis=0, tiled=True)


def body(scalar, velocity, diffusivity, recv_owner, donor_elem, recv_point, recv_coords):
    rows = recv_owner.shape[0]
    field = (2, 512, 128)
    face = (2, 64, 128)
    start = scalar.reshape(field)
    flow = velocity.reshape((3,) + field)
    nu = diffusivity.reshape(2, 128)
    owner = recv_owner.reshape(1, rows)
    donor = donor_elem.reshape(1, rows)
    point = recv_point.reshape(1, rows)
    deep = jnp.asarray(block_matrix(DERIV))
    deep_t = jnp.asarray(block_matrix(DERIV_T))

    payload, rank = call(
        query_kernel, [((128, 128), f32), ((1, rows), i32)], (owner, donor, recv_coords)
    )
    received = exchange(payload)

    ix, iy = lax.axis_index("gx"), lax.axis_index("gy")
    inside = [ix > 0, ix < lax.axis_size("gx") - 1, iy > 0, iy < lax.axis_size("gy") - 1]
    flags = jnp.where(jnp.stack(inside), 0.5, 1.0).astype(f32)
    load, inv = call(
        prepare_kernel, [(field, f32), ((512, 128), f32)], (flags, point), smem_first=True
    )
    weights_scratch = [pltpu.VMEM((8, 32, 128), f32), pltpu.VMEM((8, 32, 128), f32), pltpu.VMEM((32, 8, 128), f32)]

    def local(u):
        return call(
            local_kernel,
            [(field, f32)],
            (u, flow, nu, load, deep, deep_t),
            [pltpu.VMEM(field, f32)] * 3,
        )[0]

    def gather_faces(replies, loc):
        v, xl, xr, yl, yr = call(
            penalty_kernel,
            [(field, f32)] + [(face, f32)] * 4,
            (replies, owner, rank, point, loc),
        )
        xn = passed_along(xl, "gx", -1)
        xp = passed_along(xr, "gx", 1)
        yl, yr = call(edge_kernel, [(face, f32)] * 2, (yl, yr, xn, xp))
        yn = passed_along(yl, "gy", -1)
        yp = passed_along(yr, "gy", 1)
        return v, xn, xp, yn, yp

    u = start
    loc = local(u)
    answers = call(first_kernel, [((128, 128), f32)], (u, received), weights_scratch)[0]
    for blend in (None, (0.75, 0.25)):
        replies = exchange(answers)
        parts = gather_faces(replies, loc)
        u, answers = call(
            lambda *refs, blend=blend: step_kernel(blend, *refs),
            [(field, f32), ((128, 128), f32)],
            parts + (inv, start, u, received),
            [pltpu.VMEM(field, f32)] + weights_scratch,
        )
        loc = local(u)
    replies = exchange(answers)
    parts = gather_faces(replies, loc)
    third = call(
        lambda *refs: last_kernel((1.0 / 3.0, 2.0 / 3.0), *refs),
        [(field, f32)],
        parts + (inv, start, u),
        [pltpu.VMEM(field, f32)],
    )[0]
    return third.reshape(scalar.shape)


def solution(mesh):
    return jax.shard_map(
        body,
        mesh=mesh,
        in_specs=(
            P(None, None, "gx", "gy", None),
            P(None, None, None, "gx", "gy", None),
            P(None, "gx", "gy", None),
            P(("gx", "gy"), None),
            P(("gx", "gy")),
            P(("gx", "gy")),
            P(None, ("gx", "gy")),
        ),
        out_specs=P(None, None, "gx", "gy", None),
        check_vma=False,
    )
```

```python
import jax
import jax.numpy as jnp
import numpy as np
from jax import lax
from jax.experimental import pallas as pl
from jax.experimental.pallas import tpu as pltpu
from jax.sharding import PartitionSpec as P

time_step = 0.01
penalty_rate = 50.0
metric = 2.0
volume_factor = 0.125
node_inner = [0.8717401485096066, 0.5917001814331423, 0.20929921790247888]
f32 = jnp.float32
bf16 = jnp.bfloat16
i32 = jnp.int32


def legendre_seven(point):
    before, current = (1.0, point)
    for order in range(1, 7):
        before, current = (
            current,
            ((2 * order + 1) * point * current - order * before) / (order + 1),
        )
    return current


def gll_tables():
    degree = 7
    gll_nodes = [-1.0] + [-v for v in node_inner] + node_inner[::-1] + [1.0]
    end_values = [legendre_seven(v) for v in gll_nodes]
    weights = [2.0 / (degree * (degree + 1) * v * v) for v in end_values]
    derivative = [[0.0] * 8 for _ in range(8)]
    for a in range(8):
        for b in range(8):
            if a != b:
                derivative[a][b] = end_values[a] / (end_values[b] * (gll_nodes[a] - gll_nodes[b]))
    derivative[0][0] = -degree * (degree + 1) / 4.0
    derivative[7][7] = degree * (degree + 1) / 4.0
    return (gll_nodes, weights, derivative)


NODES, WEIGHTS, DERIV = gll_tables()
DERIV_T = [[DERIV[b][a] for b in range(8)] for a in range(8)]


def split_two(x):
    hi = x.astype(bf16)
    lo = (x - hi.astype(f32)).astype(bf16)
    return hi, lo


def block_matrix(table):
    full = np.kron(np.eye(16), np.asarray(table, np.float64)).astype(np.float32)
    hi = full.astype(jnp.bfloat16)
    lo = (full - hi.astype(np.float32)).astype(jnp.bfloat16)
    return np.concatenate([hi, lo, hi], axis=1)


def apply_table(table, pieces):
    even = [pieces[b] + pieces[7 - b] for b in range(4)]
    odd = [pieces[b] - pieces[7 - b] for b in range(4)]
    outs = [None] * 8
    for a in range(4):
        s = None
        d = None
        for b in range(4):
            cs = 0.5 * (table[a][b] - table[a][7 - b])
            cd = 0.5 * (table[a][b] + table[a][7 - b])
            s = cs * odd[b] if s is None else s + cs * odd[b]
            d = cd * even[b] if d is None else d + cd * even[b]
        outs[a] = d + s
        outs[7 - a] = s - d
    return outs


def dot_nn(a, b):
    return lax.dot_general(a, b, (((1,), (0,)), ((), ())), preferred_element_type=f32)


def dot_nt(a, b):
    return lax.dot_general(a, b, (((1,), (1,)), ((), ())), preferred_element_type=f32)


def one_hot_rows(row, count, dtype=bf16):
    ids = lax.broadcasted_iota(i32, (count, row.shape[-1]), 0)
    return jnp.where(ids == row, 1.0, 0.0).astype(dtype)


def weight_rows():
    k = lax.broadcasted_iota(i32, (8, 128), 0)
    out = jnp.zeros((8, 128), f32)
    for j in range(8):
        out = jnp.where(k == j, WEIGHTS[j], out)
    return out


def start_copies(pairs, sems):
    copies = [pltpu.make_async_copy(src, dst, sems.at[n]) for n, (src, dst) in enumerate(pairs)]
    for copy in copies:
        copy.start()
    return copies


def query_kernel(owner_any, donor_any, coords_any, payload_ref, rank_any, owner_ref, donor_ref, coords_ref, rank_ref, sems):
    copies = start_copies(
        [(owner_any, owner_ref), (donor_any, donor_ref), (coords_any, coords_ref)], sems
    )
    copies[0].wait()
    rows = owner_ref.shape[1]
    half = rows // 2
    owner = owner_ref[...]
    step = 256
    before = (
        lax.broadcasted_iota(i32, (step, step), 0) < lax.broadcasted_iota(i32, (step, step), 1)
    )
    before = jnp.where(before, 1.0, 0.0).astype(bf16)
    total = jnp.zeros((128, 1), f32)
    hots = []
    ranks = []
    for c in range(rows // step):
        sl = slice(c * step, (c + 1) * step)
        oh = one_hot_rows(owner[:, sl], 128)
        ohf = oh.astype(f32)
        cum = dot_nn(oh, before) + total
        total = total + jnp.sum(ohf, axis=1, keepdims=True)
        rank = jnp.sum(cum * ohf, axis=0, keepdims=True).astype(i32)
        rank_ref[:, sl] = rank
        hots.append(oh)
        ranks.append(rank)
    out = pltpu.make_async_copy(rank_ref, rank_any, sems.at[3])
    out.start()
    copies[1].wait()
    copies[2].wait()
    acc = [jnp.zeros((128, 128), f32) for _ in range(3)]
    for c in range(rows // step):
        sl = slice(c * step, (c + 1) * step)
        pick = lax.broadcasted_iota(i32, (32, step), 0) == ranks[c]
        col = lax.broadcasted_iota(i32, (1, step), 1) + c * step
        ident = (jnp.where(col < half, 128, 0) + donor_ref[:, sl]).astype(f32)
        parts = [[], [], []]
        for v in range(3):
            x = coords_ref[v : v + 1, sl]
            hi = x.astype(bf16).astype(f32)
            rest = x - hi
            mid = rest.astype(bf16).astype(f32)
            for p, val in enumerate((hi, mid, rest - mid)):
                parts[p].append(jnp.where(pick, val, 0.0).astype(bf16))
        zero = jnp.zeros((32, step), bf16)
        parts[0].append(jnp.where(pick, ident, 0.0).astype(bf16))
        parts[1].append(zero)
        parts[2].append(zero)
        for p in range(3):
            acc[p] = acc[p] + dot_nt(hots[c], jnp.concatenate(parts[p], axis=0))
    payload_ref[...] = acc[0] + (acc[1] + acc[2])
    out.wait()


def prepare_kernel(flags_ref, owner_any, rank_any, point_any, load_any, inv_any, table_any, mask_any,
                   load_ref, inv_ref, table_ref, mask_ref, sems):
    copies = start_copies(
        [(owner_any, table_ref.at[0]), (rank_any, table_ref.at[1]), (point_any, table_ref.at[2])], sems
    )
    for n in range(4):
        mask_ref[n] = jnp.full((8, 128), 2.0 - 2.0 * flags_ref[n], f32)
    for copy in copies:
        copy.wait()
    point_ref = table_ref.at[2]
    half = point_ref.shape[1] // 2
    wk = weight_rows()
    for m in range(2):
        point = point_ref[:, m * half : (m + 1) * half]
        q = lax.shift_right_logical(point, 7)
        e = lax.bitwise_and(point, 127)
        count = dot_nt(one_hot_rows(q, 512), one_hot_rows(e, 128))
        for ij in range(64):
            c = penalty_rate * volume_factor * WEIGHTS[ij // 8] * WEIGHTS[ij % 8]
            load_ref[m, ij * 8 : ij * 8 + 8, :] = (c * wk) * count[ij * 8 : ij * 8 + 8, :]
    k = lax.broadcasted_iota(i32, (8, 128), 0)
    e = lax.broadcasted_iota(i32, (8, 128), 1)
    shared = ((k == 0) & (e > 0)) | ((k == 7) & (e < 127))
    base = time_step / (volume_factor * wk * jnp.where(shared, 2.0, 1.0))
    for ij in range(64):
        i, j = ij // 8, ij % 8
        val = base * (1.0 / (WEIGHTS[i] * WEIGHTS[j]))
        if i == 0:
            val = val * flags_ref[0]
        if i == 7:
            val = val * flags_ref[1]
        if j == 0:
            val = val * flags_ref[2]
        if j == 7:
            val = val * flags_ref[3]
        inv_ref[ij * 8 : ij * 8 + 8, :] = val
    copies = start_copies(
        [(load_ref, load_any), (inv_ref, inv_any), (table_ref, table_any), (mask_ref, mask_any)], sems
    )
    for copy in copies:
        copy.wait()


def local_kernel(u_any, vel_any, nu_any, load_any, deep_any, table_any, mask_any, out_ref, table_ref, mask_ref, u_ref, vel_ref, nu_ref, load_ref, deep_ref,
                 ax_ref, ay_ref, fz_ref, sems):
    copies = start_copies(
        [(u_any, u_ref), (deep_any, deep_ref), (nu_any, nu_ref), (vel_any, vel_ref), (load_any, load_ref),
         (table_any, table_ref), (mask_any, mask_ref)],
        sems,
    )
    wk = weight_rows()
    copies[0].wait()
    copies[1].wait()

    def depth(table, pick):
        chunks = []
        for c in range(4):
            rows = slice(c * 128, (c + 1) * 128)
            hi, lo = split_two(jnp.concatenate([pick(0, rows), pick(1, rows)], axis=1))
            chunks.append(dot_nn(table, jnp.concatenate([hi, hi, lo], axis=0)))
        return chunks

    az = depth(deep_ref[0], lambda m, rows: u_ref[m, rows, :])
    for m in range(2):
        for j in range(8):
            outs = apply_table(DERIV, [u_ref[m, i * 64 + j * 8 : i * 64 + j * 8 + 8, :] for i in range(8)])
            for i in range(8):
                ax_ref[m, i * 64 + j * 8 : i * 64 + j * 8 + 8, :] = outs[i]
    for copy in copies[2:]:
        copy.wait()
    for m in range(2):
        wnu = 4.0 * volume_factor * wk * nu_ref[m : m + 1, :]
        wad = 2.0 * volume_factor * wk
        for i in range(8):
            outs = apply_table(DERIV, [u_ref[m, i * 64 + j * 8 : i * 64 + j * 8 + 8, :] for j in range(8)])
            fluxes = []
            for j in range(8):
                ij = i * 8 + j
                rows = slice(ij * 8, ij * 8 + 8)
                c = WEIGHTS[i] * WEIGHTS[j]
                gx = ax_ref[m, rows, :]
                gy = outs[j]
                gz = az[ij // 16][(ij % 16) * 8 : (ij % 16) * 8 + 8, m * 128 : (m + 1) * 128]
                adv = vel_ref[0, m, rows, :] * gx + vel_ref[1, m, rows, :] * gy + vel_ref[2, m, rows, :] * gz
                out_ref[m, rows, :] = -((c * wad) * adv) - load_ref[m, rows, :] * u_ref[m, rows, :]
                flux = c * wnu
                ax_ref[m, rows, :] = flux * gx
                fz_ref[m, rows, :] = flux * gz
                fluxes.append(flux * gy)
            outs = apply_table(DERIV_T, fluxes)
            for j in range(8):
                rows = slice(i * 64 + j * 8, i * 64 + j * 8 + 8)
                out_ref[m, rows, :] = out_ref[m, rows, :] - outs[j]
    bz = depth(deep_ref[1], lambda m, rows: fz_ref[m, rows, :])
    for m in range(2):
        for j in range(8):
            outs = apply_table(DERIV_T, [ax_ref[m, i * 64 + j * 8 : i * 64 + j * 8 + 8, :] for i in range(8)])
            for i in range(8):
                ij = i * 8 + j
                rows = slice(ij * 8, ij * 8 + 8)
                gz = bz[ij // 16][(ij % 16) * 8 : (ij % 16) * 8 + 8, m * 128 : (m + 1) * 128]
                out_ref[m, rows, :] = (out_ref[m, rows, :] - outs[i]) - gz


def interpolate(u, received_ref, ans_ref, wx_ref, wy_ref, wz_ref):
    parts = [split_two(v) for v in u]
    cat = jnp.concatenate([parts[0][0], parts[1][0], parts[0][1], parts[1][1]], axis=1)
    turned = received_ref[...].T
    for v, ref in enumerate((wx_ref, wy_ref, wz_ref)):
        x = turned[v * 32 : v * 32 + 32, :]
        diff = [x - NODES[m] for m in range(8)]
        pre = [None] * 8
        suf = [None] * 8
        for m in range(1, 8):
            pre[m] = diff[m - 1] if pre[m - 1] is None else pre[m - 1] * diff[m - 1]
        for m in range(6, -1, -1):
            suf[m] = diff[m + 1] if suf[m + 1] is None else suf[m + 1] * diff[m + 1]
        for j in range(8):
            c = 1.0
            for m in range(8):
                if m != j:
                    c = c / (NODES[j] - NODES[m])
            w = suf[j] if pre[j] is None else (pre[j] if suf[j] is None else pre[j] * suf[j])
            w = w * c
            if ref is wz_ref:
                ref[:, j, :] = w
            else:
                ref[j] = w
    ids = turned[96:128, :].astype(i32)
    rows = []
    for g in range(16):
        hot = [one_hot_rows(ids[s : s + 1, :], 256) for s in (2 * g, 2 * g + 1)]
        hot = jnp.concatenate(hot, axis=1)
        got = dot_nn(cat, jnp.concatenate([hot, hot], axis=0))
        for b in range(2):
            s = 2 * g + b
            total = None
            for j in range(8):
                acc = None
                for i in range(8):
                    term = wx_ref[i, s : s + 1, :] * got[i * 64 + j * 8 : i * 64 + j * 8 + 8, b * 128 : (b + 1) * 128]
                    acc = term if acc is None else acc + term
                acc = acc * wy_ref[j, s : s + 1, :]
                total = acc if total is None else total + acc
            rows.append(jnp.sum(total * wz_ref[s], axis=0, keepdims=True))
    answers = jnp.concatenate(rows + [jnp.zeros((96, 128), f32)], axis=0)
    ans_ref[...] = answers.T


def first_kernel(u_any, received_ref, ans_ref, u_ref, wx_ref, wy_ref, wz_ref, sems):
    copies = start_copies([(u_any, u_ref)], sems)
    copies[0].wait()
    interpolate([u_ref[0], u_ref[1]], received_ref, ans_ref, wx_ref, wy_ref, wz_ref)


def penalty_kernel(replies_ref, table_ref, mask_ref, local_ref, out_ref, xl_ref, xr_ref, yl_ref, yr_ref):
    owner_ref, rank_ref, point_ref = table_ref.at[0], table_ref.at[1], table_ref.at[2]
    half = point_ref.shape[1] // 2
    hi, lo = split_two(replies_ref[...].T[0:32, :])
    lhs = jnp.concatenate([hi, lo], axis=1)
    wk = weight_rows()
    for m in range(2):
        sl = slice(m * half, (m + 1) * half)
        oh = one_hot_rows(owner_ref[:, sl], 128)
        got = dot_nn(lhs, jnp.concatenate([oh, oh], axis=0))
        pick = lax.broadcasted_iota(i32, (32, half), 0) == rank_ref[:, sl]
        g = jnp.sum(jnp.where(pick, got, 0.0), axis=0, keepdims=True)
        ghi = g.astype(bf16).astype(f32)
        glo = g - ghi
        point = point_ref[:, sl]
        q = lax.shift_right_logical(point, 7)
        e = lax.bitwise_and(point, 127)
        at = lax.broadcasted_iota(i32, (128, half), 0) == e
        rhs = jnp.concatenate(
            [jnp.where(at, ghi, 0.0).astype(bf16), jnp.where(at, glo, 0.0).astype(bf16)], axis=0
        )
        both = dot_nt(one_hot_rows(q, 512), rhs)
        summed = both[:, 0:128] + both[:, 128:256]
        for ij in range(64):
            rows = slice(ij * 8, ij * 8 + 8)
            i, j = ij // 8, ij % 8
            c = penalty_rate * volume_factor * WEIGHTS[i] * WEIGHTS[j]
            val = local_ref[m, rows, :] + (c * wk) * summed[rows, :]
            out_ref[m, rows, :] = val
            if i == 0:
                xl_ref[m, j * 8 : j * 8 + 8, :] = val * mask_ref[0]
            if i == 7:
                xr_ref[m, j * 8 : j * 8 + 8, :] = val * mask_ref[1]
            if j == 0:
                yl_ref[m, i * 8 : i * 8 + 8, :] = val
            if j == 7:
                yr_ref[m, i * 8 : i * 8 + 8, :] = val


def edge_kernel(yl_ref, yr_ref, xn_ref, xp_ref, mask_ref, yl_out, yr_out):
    for m in range(2):
        for src, dst, j in ((yl_ref, yl_out, 0), (yr_ref, yr_out, 7)):
            mask = mask_ref[2 if j == 0 else 3]
            for i in range(8):
                val = src[m, i * 8 : i * 8 + 8, :]
                if i == 0:
                    val = val + xp_ref[m, j * 8 : j * 8 + 8, :]
                if i == 7:
                    val = val + xn_ref[m, j * 8 : j * 8 + 8, :]
                dst[m, i * 8 : i * 8 + 8, :] = val * mask


def finish(blend, v_ref, xn_ref, xp_ref, yn_ref, yp_ref, start_ref, u_ref, inv_ref, new_ref, work_ref, copies):
    lane = lax.broadcasted_iota(i32, (64, 128), 1)
    for m in range(2):
        for ij in range(64):
            rows = slice(ij * 8, ij * 8 + 8)
            i, j = ij // 8, ij % 8
            val = v_ref[m, rows, :]
            if j == 0:
                val = val + yp_ref[m, i * 8 : i * 8 + 8, :]
            elif j == 7:
                val = val + yn_ref[m, i * 8 : i * 8 + 8, :]
            if i == 0:
                val = val + xp_ref[m, j * 8 : j * 8 + 8, :]
            elif i == 7:
                val = val + xn_ref[m, j * 8 : j * 8 + 8, :]
            work_ref[m, rows, :] = val
        left = work_ref[m, pl.ds(0, 64, stride=8), :]
        right = work_ref[m, pl.ds(7, 64, stride=8), :]
        work_ref[m, pl.ds(0, 64, stride=8), :] = left + jnp.where(lane > 0, pltpu.roll(right, 1, 1), 0.0)
        work_ref[m, pl.ds(7, 64, stride=8), :] = right + jnp.where(lane < 127, pltpu.roll(left, 127, 1), 0.0)
    for copy in copies:
        copy.wait()
    for m in range(2):
        new = u_ref[m] + inv_ref[...] * work_ref[m]
        if blend is not None:
            new = blend[0] * start_ref[m] + blend[1] * new
        new_ref[m] = new


def step_kernel(blend, v_ref, xn_ref, xp_ref, yn_ref, yp_ref, start_any, u_any, inv_any, received_any,
                new_any, ans_ref, work_ref, start_ref, u_ref, inv_ref, received_ref, new_ref,
                wx_ref, wy_ref, wz_ref, sems):
    pairs = [(u_any, u_ref), (inv_any, inv_ref), (received_any, received_ref)]
    if blend is not None:
        pairs.append((start_any, start_ref))
    copies = start_copies(pairs, sems)
    finish(blend, v_ref, xn_ref, xp_ref, yn_ref, yp_ref, start_ref, u_ref, inv_ref, new_ref, work_ref, copies)
    out = pltpu.make_async_copy(new_ref, new_any, sems.at[4])
    out.start()
    interpolate([new_ref[0], new_ref[1]], received_ref, ans_ref, wx_ref, wy_ref, wz_ref)
    out.wait()


def last_kernel(blend, v_ref, xn_ref, xp_ref, yn_ref, yp_ref, start_any, u_any, inv_any, new_ref,
                work_ref, start_ref, u_ref, inv_ref, sems):
    copies = start_copies([(u_any, u_ref), (inv_any, inv_ref), (start_any, start_ref)], sems)
    finish(blend, v_ref, xn_ref, xp_ref, yn_ref, yp_ref, start_ref, u_ref, inv_ref, new_ref, work_ref, copies)


PINNED = "a"
SPACES = {"v": pltpu.VMEM, "a": pltpu.HBM, "s": pltpu.SMEM}


def call(kernel, outs, ins, scratch=(), spaces="", out_spaces=""):
    return pl.pallas_call(
        kernel,
        out_shape=[SPACES[c](s, d) if c in PINNED else jax.ShapeDtypeStruct(s, d) for (s, d), c in zip(outs, out_spaces)],
        in_specs=[pl.BlockSpec(memory_space=SPACES[c]) for c in spaces],
        out_specs=[pl.BlockSpec(memory_space=SPACES[c]) for c in out_spaces],
        scratch_shapes=list(scratch),
        compiler_params=pltpu.CompilerParams(vmem_limit_bytes=24 << 20),
    )(*[pltpu.with_memory_space_constraint(x, SPACES[c]) if c in PINNED else x for x, c in zip(ins, spaces)])


def passed_around(value, axis, steps):
    count = lax.axis_size(axis)
    return lax.ppermute(value, axis, [(n, (n + steps) % count) for n in range(count)])


def exchange(x):
    return lax.all_to_all(x, ("gx", "gy"), split_axis=0, concat_axis=0, tiled=True)


def body(scalar, velocity, diffusivity, recv_owner, donor_elem, recv_point, recv_coords):
    rows = recv_owner.shape[0]
    field = (2, 512, 128)
    face = (2, 64, 128)
    start = scalar.reshape(field)
    flow = velocity.reshape((3,) + field)
    nu = diffusivity.reshape(2, 128)
    owner = recv_owner.reshape(1, rows)
    donor = donor_elem.reshape(1, rows)
    point = recv_point.reshape(1, rows)
    deep = jnp.asarray(np.stack([block_matrix(DERIV), block_matrix(DERIV_T)]))

    def vmem(shape, dtype=f32):
        return pltpu.VMEM(shape, dtype)

    def dma(count):
        return pltpu.SemaphoreType.DMA((count,))

    line = vmem((1, rows), i32)
    weights_scratch = [vmem((8, 32, 128)), vmem((8, 32, 128)), vmem((32, 8, 128))]

    payload, rank = call(
        query_kernel,
        [((128, 128), f32), ((1, rows), i32)],
        (owner, donor, recv_coords),
        [line, line, vmem((3, rows)), line, dma(4)],
        "aaa",
        "va",
    )
    received = exchange(payload)

    ix, iy = lax.axis_index("gx"), lax.axis_index("gy")
    inside = [ix > 0, ix < lax.axis_size("gx") - 1, iy > 0, iy < lax.axis_size("gy") - 1]
    flags = jnp.where(jnp.stack(inside), 0.5, 1.0).astype(f32)
    load, inv, table, mask = call(
        prepare_kernel,
        [(field, f32), ((512, 128), f32), ((3, 1, rows), i32), ((4, 8, 128), f32)],
        (flags, owner, rank, point),
        [vmem(field), vmem((512, 128)), vmem((3, 1, rows), i32), vmem((4, 8, 128)), dma(4)],
        "saaa",
        "aaaa",
    )

    def local(u):
        return call(
            local_kernel,
            [(field, f32), ((3, 1, rows), i32), ((4, 8, 128), f32)],
            (u, flow, nu, load, deep, table, mask),
            [vmem(field), vmem((3,) + field), vmem((2, 128)), vmem(field), vmem((2, 128, 384), bf16)]
            + [vmem(field)] * 3
            + [dma(7)],
            "aaaaaaa",
            "vvv",
        )

    def gather_faces(replies, loc, table, mask):
        v, xl, xr, yl, yr = call(
            penalty_kernel,
            [(field, f32)] + [(face, f32)] * 4,
            (replies, table, mask, loc),
            (),
            "vvvv",
            "vvvvv",
        )
        xn = passed_around(xl, "gx", -1)
        xp = passed_around(xr, "gx", 1)
        yl, yr = call(edge_kernel, [(face, f32)] * 2, (yl, yr, xn, xp, mask), (), "vvvvv", "vv")
        yn = passed_around(yl, "gy", -1)
        yp = passed_around(yr, "gy", 1)
        return v, xn, xp, yn, yp

    u = start
    loc = local(u)
    received, loc = lax.optimization_barrier((received, loc))
    answers = call(
        first_kernel,
        [((128, 128), f32)],
        (u, received),
        [vmem(field)] + weights_scratch + [dma(1)],
        "av",
        "v",
    )[0]
    for blend in (None, (0.75, 0.25)):
        replies = exchange(answers)
        parts = gather_faces(replies, *loc)
        u, answers = call(
            lambda *refs, blend=blend: step_kernel(blend, *refs),
            [(field, f32), ((128, 128), f32)],
            parts + (start, u, inv, received),
            [vmem(field)] * 3 + [vmem((512, 128)), vmem((128, 128)), vmem(field)] + weights_scratch + [dma(5)],
            "vvvvvaaaa",
            "av",
        )
        loc = local(u)
    replies = exchange(answers)
    parts = gather_faces(replies, *loc)
    third = call(
        lambda *refs: last_kernel((1.0 / 3.0, 2.0 / 3.0), *refs),
        [(field, f32)],
        parts + (start, u, inv),
        [vmem(field)] * 3 + [vmem((512, 128)), dma(3)],
        "vvvvvaaa",
        "v",
    )[0]
    return third.reshape(scalar.shape)


def solution(mesh):
    return jax.shard_map(
        body,
        mesh=mesh,
        in_specs=(
            P(None, None, "gx", "gy", None),
            P(None, None, None, "gx", "gy", None),
            P(None, "gx", "gy", None),
            P(("gx", "gy"), None),
            P(("gx", "gy")),
            P(("gx", "gy")),
            P(None, ("gx", "gy")),
        ),
        out_specs=P(None, None, "gx", "gy", None),
        check_vma=False,
    )
```

```python
import jax
import jax.numpy as jnp
import numpy as np
from jax import lax
from jax.experimental import pallas as pl
from jax.experimental.pallas import tpu as pltpu
from jax.sharding import PartitionSpec as P

time_step = 0.01
penalty_rate = 50.0
metric = 2.0
volume_factor = 0.125
node_inner = [0.8717401485096066, 0.5917001814331423, 0.20929921790247888]
f32 = jnp.float32
bf16 = jnp.bfloat16
i32 = jnp.int32


def legendre_seven(point):
    before, current = (1.0, point)
    for order in range(1, 7):
        before, current = (
            current,
            ((2 * order + 1) * point * current - order * before) / (order + 1),
        )
    return current


def gll_tables():
    degree = 7
    gll_nodes = [-1.0] + [-v for v in node_inner] + node_inner[::-1] + [1.0]
    end_values = [legendre_seven(v) for v in gll_nodes]
    weights = [2.0 / (degree * (degree + 1) * v * v) for v in end_values]
    derivative = [[0.0] * 8 for _ in range(8)]
    for a in range(8):
        for b in range(8):
            if a != b:
                derivative[a][b] = end_values[a] / (end_values[b] * (gll_nodes[a] - gll_nodes[b]))
    derivative[0][0] = -degree * (degree + 1) / 4.0
    derivative[7][7] = degree * (degree + 1) / 4.0
    return (gll_nodes, weights, derivative)


NODES, WEIGHTS, DERIV = gll_tables()
DERIV_T = [[DERIV[b][a] for b in range(8)] for a in range(8)]


def split_two(x):
    hi = x.astype(bf16)
    lo = (x - hi.astype(f32)).astype(bf16)
    return hi, lo


def block_matrix(table):
    full = np.kron(np.eye(16), np.asarray(table, np.float64)).astype(np.float32)
    hi = full.astype(jnp.bfloat16)
    lo = (full - hi.astype(np.float32)).astype(jnp.bfloat16)
    return np.concatenate([hi, lo, hi], axis=1)


def apply_table(table, pieces):
    even = [pieces[b] + pieces[7 - b] for b in range(4)]
    odd = [pieces[b] - pieces[7 - b] for b in range(4)]
    outs = [None] * 8
    for a in range(4):
        s = None
        d = None
        for b in range(4):
            cs = 0.5 * (table[a][b] - table[a][7 - b])
            cd = 0.5 * (table[a][b] + table[a][7 - b])
            s = cs * odd[b] if s is None else s + cs * odd[b]
            d = cd * even[b] if d is None else d + cd * even[b]
        outs[a] = d + s
        outs[7 - a] = s - d
    return outs


def dot_nn(a, b):
    return lax.dot_general(a, b, (((1,), (0,)), ((), ())), preferred_element_type=f32)


def dot_nt(a, b):
    return lax.dot_general(a, b, (((1,), (1,)), ((), ())), preferred_element_type=f32)


def one_hot_rows(row, count, dtype=bf16):
    ids = lax.broadcasted_iota(jnp.int16, (count, row.shape[-1]), 0)
    return jnp.where(ids == row.astype(jnp.int16), jnp.ones((), dtype), jnp.zeros((), dtype))


def weight_rows():
    k = lax.broadcasted_iota(i32, (8, 128), 0)
    out = jnp.zeros((8, 128), f32)
    for j in range(8):
        out = jnp.where(k == j, WEIGHTS[j], out)
    return out


def start_copies(pairs, sems):
    copies = [pltpu.make_async_copy(src, dst, sems.at[n]) for n, (src, dst) in enumerate(pairs)]
    for copy in copies:
        copy.start()
    return copies


def query_kernel(owner_any, donor_any, coords_any, payload_ref, rank_any, owner_ref, donor_ref, coords_ref, rank_ref, sems):
    copies = start_copies(
        [(owner_any, owner_ref), (donor_any, donor_ref), (coords_any, coords_ref)], sems
    )
    copies[0].wait()
    rows = owner_ref.shape[1]
    half = rows // 2
    owner = owner_ref[...]
    step = 256
    before = (
        lax.broadcasted_iota(i32, (step, step), 0) < lax.broadcasted_iota(i32, (step, step), 1)
    )
    before = jnp.where(before, 1.0, 0.0).astype(bf16)
    total = jnp.zeros((128, 1), f32)
    hots = []
    ranks = []
    for c in range(rows // step):
        sl = slice(c * step, (c + 1) * step)
        oh = one_hot_rows(owner[:, sl], 128)
        ohf = oh.astype(f32)
        cum = dot_nn(oh, before) + total
        total = total + jnp.sum(ohf, axis=1, keepdims=True)
        rank = jnp.sum(cum * ohf, axis=0, keepdims=True).astype(i32)
        rank_ref[:, sl] = rank
        hots.append(oh)
        ranks.append(rank)
    out = pltpu.make_async_copy(rank_ref, rank_any, sems.at[3])
    out.start()
    copies[1].wait()
    copies[2].wait()
    acc = [jnp.zeros((128, 128), f32) for _ in range(3)]
    for c in range(rows // step):
        sl = slice(c * step, (c + 1) * step)
        pick = lax.broadcasted_iota(i32, (32, step), 0) == ranks[c]
        col = lax.broadcasted_iota(i32, (1, step), 1) + c * step
        ident = (jnp.where(col < half, 128, 0) + donor_ref[:, sl]).astype(f32)
        parts = [[], [], []]
        for v in range(3):
            x = coords_ref[v : v + 1, sl]
            hi = x.astype(bf16).astype(f32)
            rest = x - hi
            mid = rest.astype(bf16).astype(f32)
            for p, val in enumerate((hi, mid, rest - mid)):
                parts[p].append(jnp.where(pick, val, 0.0).astype(bf16))
        zero = jnp.zeros((32, step), bf16)
        parts[0].append(jnp.where(pick, ident, 0.0).astype(bf16))
        parts[1].append(zero)
        parts[2].append(zero)
        for p in range(3):
            acc[p] = acc[p] + dot_nt(hots[c], jnp.concatenate(parts[p], axis=0))
    payload_ref[...] = acc[0] + (acc[1] + acc[2])
    out.wait()


def prepare_kernel(flags_ref, owner_any, rank_any, point_any, load_any, inv_any, table_any, mask_any, low_any, high_any,
                   load_ref, inv_ref, table_ref, mask_ref, low_ref, high_ref, sems):
    copies = start_copies(
        [(owner_any, table_ref.at[0:1]), (rank_any, table_ref.at[1:2]), (point_any, table_ref.at[2:3])], sems
    )
    for n in range(4):
        mask_ref[n] = jnp.full((8, 128), flags_ref[n], i32).astype(f32)
    for copy in copies:
        copy.wait()
    for n, ref in enumerate((low_ref, high_ref)):
        ref[0:2, :] = table_ref[0:2, :]
        ref[2:3, :] = (table_ref[2:3, :] + 1) * flags_ref[n + 2] - 1
    half = table_ref.shape[1] // 2
    wk = weight_rows()
    for m in range(2):
        point = table_ref[2:3, m * half : (m + 1) * half]
        q = lax.shift_right_logical(point, 7)
        e = lax.bitwise_and(point, 127)
        count = dot_nt(one_hot_rows(q, 512), one_hot_rows(e, 128))
        for ij in range(64):
            c = penalty_rate * volume_factor * WEIGHTS[ij // 8] * WEIGHTS[ij % 8]
            load_ref[m, ij * 8 : ij * 8 + 8, :] = (c * wk) * count[ij * 8 : ij * 8 + 8, :]
    k = lax.broadcasted_iota(i32, (8, 128), 0)
    e = lax.broadcasted_iota(i32, (8, 128), 1)
    shared = ((k == 0) & (e > 0)) | ((k == 7) & (e < 127))
    base = time_step / (volume_factor * wk * jnp.where(shared, 2.0, 1.0))
    for ij in range(64):
        i, j = ij // 8, ij % 8
        val = base * (1.0 / (WEIGHTS[i] * WEIGHTS[j]))
        if i in (0, 7):
            val = val * (1.0 - 0.5 * mask_ref[0 if i == 0 else 1])
        if j in (0, 7):
            val = val * (1.0 - 0.5 * mask_ref[2 if j == 0 else 3])
        inv_ref[ij * 8 : ij * 8 + 8, :] = val
    copies = start_copies(
        [(load_ref, load_any), (inv_ref, inv_any), (table_ref, table_any), (mask_ref, mask_any),
         (low_ref, low_any), (high_ref, high_any)],
        sems,
    )
    for copy in copies:
        copy.wait()


def relay_kernel(flags_ref, own_ref, below_ref, above_ref, low_ref, high_ref):
    for n, ref in ((0, low_ref), (1, high_ref)):
        for t, src in enumerate((own_ref, below_ref, above_ref)):
            ref[3 * t : 3 * t + 2, :] = src[0:2, :]
            ref[3 * t + 2 : 3 * t + 3, :] = (src[2:3, :] + 1) * flags_ref[n] - 1


GHOSTS = [(-1, 0), (1, 0), (0, -1), (0, 1), (-1, -1), (-1, 1), (1, -1), (1, 1)]


def ghost_kernel(xp_ref, xn_ref, yp_ref, yn_ref, out_any, out_ref, sems):
    for n, (dx, dy) in enumerate(GHOSTS):
        if dx == 0:
            src, base = (yp_ref, 0) if dy < 0 else (yn_ref, 0)
        else:
            src, base = (xp_ref if dx < 0 else xn_ref), {0: 0, -1: 3, 1: 6}[dy]
        point = src[base + 2 : base + 3, :]
        q = lax.shift_right_arithmetic(point, 7)
        i = lax.shift_right_arithmetic(q, 6)
        j = lax.bitwise_and(lax.shift_right_arithmetic(q, 3), 7)
        k = lax.bitwise_and(q, 7)
        good = point >= 0
        if dx:
            good = good & (i == (7 if dx < 0 else 0))
        if dy:
            good = good & (j == (7 if dy < 0 else 0))
        row = k if dx and dy else (j * 8 + k if dx else i * 8 + k)
        out_ref[n, 0:2, :] = src[base : base + 2, :]
        out_ref[n, 2:3, :] = jnp.where(good, row, -1)
        out_ref[n, 3:4, :] = lax.bitwise_and(point, 127)
    copies = start_copies([(out_ref, out_any)], sems)
    copies[0].wait()


def local_rates(u_ref, vel_ref, nu_ref, load_ref, deep_ref, out_ref, ax_ref, ay_ref, fz_ref, copies):
    wk = weight_rows()

    def depth(table, pick):
        chunks = []
        for c in range(4):
            rows = slice(c * 128, (c + 1) * 128)
            hi, lo = split_two(jnp.concatenate([pick(0, rows), pick(1, rows)], axis=1))
            chunks.append(dot_nn(table, jnp.concatenate([hi, hi, lo], axis=0)))
        return chunks

    az = depth(deep_ref[0], lambda m, rows: u_ref[m, rows, :])
    for m in range(2):
        for j in range(8):
            outs = apply_table(DERIV, [u_ref[m, i * 64 + j * 8 : i * 64 + j * 8 + 8, :] for i in range(8)])
            for i in range(8):
                ax_ref[m, i * 64 + j * 8 : i * 64 + j * 8 + 8, :] = outs[i]
    for copy in copies:
        copy.wait()
    for m in range(2):
        wnu = 4.0 * volume_factor * wk * nu_ref[m : m + 1, :]
        wad = 2.0 * volume_factor * wk
        for i in range(8):
            outs = apply_table(DERIV, [u_ref[m, i * 64 + j * 8 : i * 64 + j * 8 + 8, :] for j in range(8)])
            fluxes = []
            for j in range(8):
                ij = i * 8 + j
                rows = slice(ij * 8, ij * 8 + 8)
                c = WEIGHTS[i] * WEIGHTS[j]
                gx = ax_ref[m, rows, :]
                gy = outs[j]
                gz = az[ij // 16][(ij % 16) * 8 : (ij % 16) * 8 + 8, m * 128 : (m + 1) * 128]
                adv = vel_ref[0, m, rows, :] * gx + vel_ref[1, m, rows, :] * gy + vel_ref[2, m, rows, :] * gz
                out_ref[m, rows, :] = -((c * wad) * adv) - load_ref[m, rows, :] * u_ref[m, rows, :]
                flux = c * wnu
                ax_ref[m, rows, :] = flux * gx
                fz_ref[m, rows, :] = flux * gz
                fluxes.append(flux * gy)
            outs = apply_table(DERIV_T, fluxes)
            for j in range(8):
                rows = slice(i * 64 + j * 8, i * 64 + j * 8 + 8)
                out_ref[m, rows, :] = out_ref[m, rows, :] - outs[j]
    bz = depth(deep_ref[1], lambda m, rows: fz_ref[m, rows, :])
    for m in range(2):
        for j in range(8):
            outs = apply_table(DERIV_T, [ax_ref[m, i * 64 + j * 8 : i * 64 + j * 8 + 8, :] for i in range(8)])
            for i in range(8):
                ij = i * 8 + j
                rows = slice(ij * 8, ij * 8 + 8)
                gz = bz[ij // 16][(ij % 16) * 8 : (ij % 16) * 8 + 8, m * 128 : (m + 1) * 128]
                out_ref[m, rows, :] = (out_ref[m, rows, :] - outs[i]) - gz


def send_faces(loc_ref, mask_ref, xl_ref, xr_ref, yl_ref, yr_ref, keep_ref):
    for m in range(2):
        for n in range(8):
            rows = slice(n * 8, n * 8 + 8)
            xl_ref[m, rows, :] = loc_ref[m, rows, :]
            xr_ref[m, rows, :] = loc_ref[m, 448 + n * 8 : 456 + n * 8, :]
            yl_ref[m, rows, :] = loc_ref[m, n * 64 : n * 64 + 8, :] * mask_ref[2]
            yr_ref[m, rows, :] = loc_ref[m, n * 64 + 56 : n * 64 + 64, :] * mask_ref[3]
    keep_ref[...] = mask_ref[0:2]


def local_kernel(u_any, vel_any, nu_any, load_any, deep_any, mask_any, loc_ref, xl_ref, xr_ref, yl_ref, yr_ref, keep_ref,
                 u_ref, vel_ref, nu_ref, load_ref, deep_ref, mask_ref, ax_ref, ay_ref, fz_ref, sems):
    copies = start_copies(
        [(u_any, u_ref), (deep_any, deep_ref), (nu_any, nu_ref), (vel_any, vel_ref), (load_any, load_ref),
         (mask_any, mask_ref)],
        sems,
    )
    copies[0].wait()
    copies[1].wait()
    local_rates(u_ref, vel_ref, nu_ref, load_ref, deep_ref, loc_ref, ax_ref, ay_ref, fz_ref, copies[2:])
    send_faces(loc_ref, mask_ref, xl_ref, xr_ref, yl_ref, yr_ref, keep_ref)


def interpolate(u, received_ref, ans_ref, wx_ref, wy_ref, wz_ref, copies):
    parts = [split_two(v) for v in u]
    cat = jnp.concatenate([parts[0][0], parts[1][0], parts[0][1], parts[1][1]], axis=1)
    for copy in copies:
        copy.wait()
    turned = received_ref[...].T
    for v, ref in enumerate((wx_ref, wy_ref, wz_ref)):
        x = turned[v * 32 : v * 32 + 32, :]
        diff = [x - NODES[m] for m in range(8)]
        pre = [None] * 8
        suf = [None] * 8
        for m in range(1, 8):
            pre[m] = diff[m - 1] if pre[m - 1] is None else pre[m - 1] * diff[m - 1]
        for m in range(6, -1, -1):
            suf[m] = diff[m + 1] if suf[m + 1] is None else suf[m + 1] * diff[m + 1]
        for j in range(8):
            c = 1.0
            for m in range(8):
                if m != j:
                    c = c / (NODES[j] - NODES[m])
            w = suf[j] if pre[j] is None else (pre[j] if suf[j] is None else pre[j] * suf[j])
            w = w * c
            if ref is wz_ref:
                ref[:, j, :] = w
            else:
                ref[j] = w
    ids = turned[96:128, :].astype(i32)
    rows = []
    for g in range(16):
        hot = [one_hot_rows(ids[s : s + 1, :], 256) for s in (2 * g, 2 * g + 1)]
        hot = jnp.concatenate(hot, axis=1)
        got = dot_nn(cat, jnp.concatenate([hot, hot], axis=0))
        for b in range(2):
            s = 2 * g + b
            total = None
            for j in range(8):
                acc = None
                for i in range(8):
                    term = wx_ref[i, s : s + 1, :] * got[i * 64 + j * 8 : i * 64 + j * 8 + 8, b * 128 : (b + 1) * 128]
                    acc = term if acc is None else acc + term
                acc = acc * wy_ref[j, s : s + 1, :]
                total = acc if total is None else total + acc
            rows.append(jnp.sum(total * wz_ref[s], axis=0, keepdims=True))
    answers = jnp.concatenate(rows, axis=0)
    blocks = [answers]
    for dx, dy in GHOSTS:
        blocks.append(pltpu.roll(answers, (-(4 * dx + dy)) % 128, 1))
    for a in range(3):
        group = blocks[4 * a : 4 * a + 4]
        if len(group) < 4:
            group = group + [jnp.zeros((32 * (4 - len(group)), 128), f32)]
        ans_ref[:, a, :] = jnp.concatenate(group, axis=0).T
    ans_ref[:, 3, :] = jnp.zeros((128, 128), f32)


def answer_kernel(u_ref, received_any, ans_ref, received_ref, wx_ref, wy_ref, wz_ref, sems):
    copies = start_copies([(received_any, received_ref)], sems)
    interpolate([u_ref[0], u_ref[1]], received_ref, ans_ref, wx_ref, wy_ref, wz_ref, copies)


def first_kernel(u_any, received_ref, ans_ref, u_ref, wx_ref, wy_ref, wz_ref, sems):
    copies = start_copies([(u_any, u_ref)], sems)
    copies[0].wait()
    interpolate([u_ref[0], u_ref[1]], received_ref, ans_ref, wx_ref, wy_ref, wz_ref, [])


def edge_kernel(xl_ref, xr_ref, yn_ref, yp_ref, keep_ref, xl_out, xr_out):
    for m in range(2):
        for src, dst, i in ((xl_ref, xl_out, 0), (xr_ref, xr_out, 7)):
            mask = keep_ref[0 if i == 0 else 1]
            for j in range(8):
                val = src[m, j * 8 : j * 8 + 8, :]
                if j == 0:
                    val = val + yp_ref[m, i * 8 : i * 8 + 8, :]
                if j == 7:
                    val = val + yn_ref[m, i * 8 : i * 8 + 8, :]
                dst[m, j * 8 : j * 8 + 8, :] = val * mask


def bring_kernel(after_ref, table_any, ghost_any, table_ref, ghost_ref, sems):
    copies = start_copies([(table_any, table_ref), (ghost_any, ghost_ref)], sems)
    for copy in copies:
        copy.wait()


def with_faces(parts, m, ij):
    loc_ref, xn_ref, xp_ref, yn_ref, yp_ref = parts
    i, j = ij // 8, ij % 8
    val = loc_ref[m, ij * 8 : ij * 8 + 8, :]
    if j == 0:
        val = val + yp_ref[m, i * 8 : i * 8 + 8, :]
    elif j == 7:
        val = val + yn_ref[m, i * 8 : i * 8 + 8, :]
    if i == 0:
        val = val + xp_ref[m, j * 8 : j * 8 + 8, :]
    elif i == 7:
        val = val + xn_ref[m, j * 8 : j * 8 + 8, :]
    return val


def picked(block, owner, rank):
    parts = []
    for c in range(owner.shape[1] // 128):
        sl = slice(c * 128, (c + 1) * 128)
        index = jnp.broadcast_to(owner[:, sl], (32, 128))
        got = jnp.take_along_axis(block, index, axis=1, mode="promise_in_bounds")
        pick = lax.broadcasted_iota(i32, (32, 128), 0) == rank[:, sl]
        parts.append(jnp.sum(jnp.where(pick, got, 0.0), axis=0, keepdims=True))
    g = jnp.concatenate(parts, axis=1)
    ghi = g.astype(bf16).astype(f32)
    return ghi, g - ghi


def add_replies(replies_ref, table_ref, ghost_ref, parts, work_ref):
    half = table_ref.shape[1] // 2
    wk = weight_rows()
    blocks = []
    for a in range(3):
        turned = replies_ref[:, a, :].T
        for c in range(4):
            if 4 * a + c < 9:
                blocks.append(turned[c * 32 : c * 32 + 32, :])
    for m in range(2):
        sl = slice(m * half, (m + 1) * half)
        faces = {}
        for n, where in enumerate(GHOSTS):
            ghi, glo = picked(blocks[n + 1], ghost_ref[n, 0:1, sl], ghost_ref[n, 1:2, sl])
            size = 8 if where[0] and where[1] else 64
            at = lax.broadcasted_iota(i32, (size, half), 0) == ghost_ref[n, 2:3, sl]
            lhs = jnp.concatenate([jnp.where(at, ghi, 0.0), jnp.where(at, glo, 0.0)], axis=0).astype(bf16)
            both = dot_nt(lhs, one_hot_rows(ghost_ref[n, 3:4, sl], 128))
            faces[where] = both[0:size, :] + both[size : 2 * size, :]
        ghi, glo = picked(blocks[0], table_ref[0:1, sl], table_ref[1:2, sl])
        point = table_ref[2:3, sl]
        q = lax.shift_right_logical(point, 7)
        e = lax.bitwise_and(point, 127)
        at = lax.broadcasted_iota(i32, (128, half), 0) == e
        rhs = jnp.concatenate(
            [jnp.where(at, ghi, 0.0).astype(bf16), jnp.where(at, glo, 0.0).astype(bf16)], axis=0
        )
        both = dot_nt(one_hot_rows(q, 512), rhs)
        summed = both[:, 0:128] + both[:, 128:256]
        for ij in range(64):
            rows = slice(ij * 8, ij * 8 + 8)
            i, j = ij // 8, ij % 8
            dx = {0: -1, 7: 1}.get(i, 0)
            dy = {0: -1, 7: 1}.get(j, 0)
            c = penalty_rate * volume_factor * WEIGHTS[i] * WEIGHTS[j]
            g = summed[rows, :]
            if dx:
                g = g + faces[(dx, 0)][j * 8 : j * 8 + 8, :]
            if dy:
                g = g + faces[(0, dy)][i * 8 : i * 8 + 8, :]
            if dx and dy:
                g = g + faces[(dx, dy)]
            work_ref[m, rows, :] = with_faces(parts, m, ij) + (c * wk) * g


def advance(blend, start_ref, u_ref, inv_ref, work_ref, new_ref):
    lane = lax.broadcasted_iota(i32, (64, 128), 1)
    for m in range(2):
        left = work_ref[m, pl.ds(0, 64, stride=8), :]
        right = work_ref[m, pl.ds(7, 64, stride=8), :]
        work_ref[m, pl.ds(0, 64, stride=8), :] = left + jnp.where(lane > 0, pltpu.roll(right, 1, 1), 0.0)
        work_ref[m, pl.ds(7, 64, stride=8), :] = right + jnp.where(lane < 127, pltpu.roll(left, 127, 1), 0.0)
        new = u_ref[m] + inv_ref[...] * work_ref[m]
        if blend is not None:
            new = blend[0] * start_ref[m] + blend[1] * new
        new_ref[m] = new


def step_kernel(blend, replies_ref, table_ref, ghost_ref, old_ref, xn_ref, xp_ref, yn_ref, yp_ref, start_any, u_any, inv_any, vel_any, nu_any, load_any,
                deep_any, mask_any, new_any, new_ref, loc_ref, xl_ref, xr_ref, yl_ref, yr_ref, keep_ref,
                work_ref, start_ref, u_ref, inv_ref, vel_ref, nu_ref, load_ref, deep_ref, mask_ref,
                ax_ref, ay_ref, fz_ref, sems):
    copies = start_copies(
        [(u_any, u_ref), (inv_any, inv_ref), (start_any, start_ref), (deep_any, deep_ref), (nu_any, nu_ref),
         (vel_any, vel_ref), (load_any, load_ref), (mask_any, mask_ref)],
        sems,
    )
    add_replies(replies_ref, table_ref, ghost_ref, (old_ref, xn_ref, xp_ref, yn_ref, yp_ref), work_ref)
    for copy in copies[:4]:
        copy.wait()
    advance(blend, start_ref, u_ref, inv_ref, work_ref, new_ref)
    out = pltpu.make_async_copy(new_ref, new_any, sems.at[8])
    out.start()
    local_rates(new_ref, vel_ref, nu_ref, load_ref, deep_ref, loc_ref, ax_ref, ay_ref, fz_ref, copies[4:])
    send_faces(loc_ref, mask_ref, xl_ref, xr_ref, yl_ref, yr_ref, keep_ref)
    out.wait()


def last_kernel(blend, replies_ref, table_ref, ghost_ref, old_ref, xn_ref, xp_ref, yn_ref, yp_ref, start_any, u_any, inv_any, new_ref,
                work_ref, start_ref, u_ref, inv_ref, sems):
    copies = start_copies([(u_any, u_ref), (inv_any, inv_ref), (start_any, start_ref)], sems)
    add_replies(replies_ref, table_ref, ghost_ref, (old_ref, xn_ref, xp_ref, yn_ref, yp_ref), work_ref)
    for copy in copies:
        copy.wait()
    advance(blend, start_ref, u_ref, inv_ref, work_ref, new_ref)


PINNED = "ap"
SPACES = {"p": pltpu.VMEM, "v": pltpu.VMEM, "a": pltpu.HBM, "s": pltpu.SMEM}


def call(kernel, outs, ins, scratch=(), spaces="", out_spaces=""):
    return pl.pallas_call(
        kernel,
        out_shape=[SPACES[c](s, d) if c in PINNED else jax.ShapeDtypeStruct(s, d) for (s, d), c in zip(outs, out_spaces)],
        in_specs=[pl.BlockSpec(memory_space=SPACES[c]) for c in spaces],
        out_specs=[pl.BlockSpec(memory_space=SPACES[c]) for c in out_spaces],
        scratch_shapes=list(scratch),
        compiler_params=pltpu.CompilerParams(vmem_limit_bytes=28 << 20),
    )(*[pltpu.with_memory_space_constraint(x, SPACES[c]) if c in PINNED else x for x, c in zip(ins, spaces)])


def passed_around(value, axis, steps):
    count = lax.axis_size(axis)
    return lax.ppermute(value, axis, [(n, (n + steps) % count) for n in range(count)])


def exchange(x):
    return lax.all_to_all(x, ("gx", "gy"), split_axis=0, concat_axis=0, tiled=True)


def body(scalar, velocity, diffusivity, recv_owner, donor_elem, recv_point, recv_coords):
    rows = recv_owner.shape[0]
    field = (2, 512, 128)
    face = (2, 64, 128)
    start = scalar.reshape(field)
    flow = velocity.reshape((3,) + field)
    nu = diffusivity.reshape(2, 128)
    owner = recv_owner.reshape(1, rows)
    donor = donor_elem.reshape(1, rows)
    point = recv_point.reshape(1, rows)
    deep = jnp.asarray(np.stack([block_matrix(DERIV), block_matrix(DERIV_T)]))

    def vmem(shape, dtype=f32):
        return pltpu.VMEM(shape, dtype)

    def dma(count):
        return pltpu.SemaphoreType.DMA((count,))

    line = vmem((1, rows), i32)
    weights_scratch = [vmem((8, 32, 128)), vmem((8, 32, 128)), vmem((32, 8, 128))]
    local_scratch = [vmem((3,) + field), vmem((2, 128)), vmem(field), vmem((2, 128, 384), bf16), vmem((4, 8, 128))]
    local_scratch = local_scratch + [vmem(field)] * 3
    tables = [((3, rows), i32)] * 2

    payload, rank = call(
        query_kernel,
        [((128, 128), f32), ((1, rows), i32)],
        (owner, donor, recv_coords),
        [line, line, vmem((3, rows)), line, dma(4)],
        "aaa",
        "va",
    )
    received = exchange(payload)

    ix, iy = lax.axis_index("gx"), lax.axis_index("gy")
    inside = [ix > 0, ix < lax.axis_size("gx") - 1, iy > 0, iy < lax.axis_size("gy") - 1]
    flags = jnp.stack(inside).astype(i32)
    load, inv, table, mask, low, high = call(
        prepare_kernel,
        [(field, f32), ((512, 128), f32), ((3, rows), i32), ((4, 8, 128), f32)] + tables,
        (flags, owner, rank, point),
        [vmem(field), vmem((512, 128)), vmem((3, rows), i32), vmem((4, 8, 128))]
        + [vmem((3, rows), i32)] * 2
        + [dma(6)],
        "saaa",
        "aaaaaa",
    )

    def along_y(yl, yr):
        return passed_around(yl, "gy", -1), passed_around(yr, "gy", 1)

    def along_x(xl, xr, yn, yp, keep):
        xl, xr = call(edge_kernel, [(face, f32)] * 2, (xl, xr, yn, yp, keep), (), "vvvvv", "vv")
        return passed_around(xl, "gx", -1), passed_around(xr, "gx", 1)

    def bring(after):
        return call(
            bring_kernel,
            [((3, rows), i32), ((8, 4, rows), i32)],
            (after, table, ghosts),
            [dma(2)],
            "vaa",
            "vv",
        )

    outs = [(field, f32)] + [(face, f32)] * 4 + [((2, 8, 128), f32)]
    u = start
    loc, xl, xr, yl, yr, keep = call(
        local_kernel,
        outs,
        (u, flow, nu, load, deep, mask),
        [vmem(field)] + local_scratch + [dma(6)],
        "aaaaaa",
        "vvvvvv",
    )
    received, loc, yl, yr, low, high = lax.optimization_barrier((received, loc, yl, yr, low, high))
    yn, yp = along_y(yl, yr)
    table_n, table_p = along_y(low, high)
    answers = call(
        first_kernel,
        [((128, 4, 128), f32)],
        (u, received),
        [vmem(field)] + weights_scratch + [dma(1)],
        "av",
        "p",
    )[0]
    answers, yn, yp, table_n, table_p = lax.optimization_barrier((answers, yn, yp, table_n, table_p))
    replies = exchange(answers)
    xn, xp = along_x(xl, xr, yn, yp, keep)
    low, high = call(
        relay_kernel, [((9, rows), i32)] * 2, (flags, table, table_p, table_n), (), "svvv", "vv"
    )
    tables_n, tables_p = passed_around(low, "gx", -1), passed_around(high, "gx", 1)
    ghosts = call(
        ghost_kernel,
        [((8, 4, rows), i32)],
        (tables_p, tables_n, table_p, table_n),
        [vmem((8, 4, rows), i32), dma(1)],
        "vvvv",
        "a",
    )[0]
    own, near = bring(keep)
    for blend in (None, (0.75, 0.25)):
        u, near_u, loc, xl, xr, yl, yr, keep = call(
            lambda *refs, blend=blend: step_kernel(blend, *refs),
            [(field, f32)] * 2 + outs,
            (replies, own, near, loc, xn, xp, yn, yp, start, u, inv, flow, nu, load, deep, mask),
            [vmem(field)] * 3 + [vmem((512, 128))] + local_scratch + [dma(9)],
            "vvvvvvvvaaaaaaaa",
            "avvvvvvv",
        )
        yn, yp = along_y(yl, yr)
        answers = call(
            answer_kernel,
            [((128, 4, 128), f32)],
            (near_u, received),
            [vmem((128, 128))] + weights_scratch + [dma(1)],
            "va",
            "p",
        )[0]
        answers, yn, yp = lax.optimization_barrier((answers, yn, yp))
        replies = exchange(answers)
        xn, xp = along_x(xl, xr, yn, yp, keep)
        own, near = bring(keep)
    third = call(
        lambda *refs: last_kernel((1.0 / 3.0, 2.0 / 3.0), *refs),
        [(field, f32)],
        (replies, own, near, loc, xn, xp, yn, yp, start, u, inv),
        [vmem(field)] * 3 + [vmem((512, 128)), dma(3)],
        "vvvvvvvvaaa",
        "v",
    )[0]
    return third.reshape(scalar.shape)


def solution(mesh):
    return jax.shard_map(
        body,
        mesh=mesh,
        in_specs=(
            P(None, None, "gx", "gy", None),
            P(None, None, None, "gx", "gy", None),
            P(None, "gx", "gy", None),
            P(("gx", "gy"), None),
            P(("gx", "gy")),
            P(("gx", "gy")),
            P(None, ("gx", "gy")),
        ),
        out_specs=P(None, None, "gx", "gy", None),
        check_vma=False,
    )
```

```python
import jax
import jax.numpy as jnp
import numpy as np
from jax import lax
from jax.experimental import pallas as pl
from jax.experimental.pallas import tpu as pltpu
from jax.sharding import PartitionSpec as P

time_step = 0.01
penalty_rate = 50.0
metric = 2.0
volume_factor = 0.125
node_inner = [0.8717401485096066, 0.5917001814331423, 0.20929921790247888]
f32 = jnp.float32
bf16 = jnp.bfloat16
i32 = jnp.int32


def legendre_seven(point):
    before, current = (1.0, point)
    for order in range(1, 7):
        before, current = (
            current,
            ((2 * order + 1) * point * current - order * before) / (order + 1),
        )
    return current


def gll_tables():
    degree = 7
    gll_nodes = [-1.0] + [-v for v in node_inner] + node_inner[::-1] + [1.0]
    end_values = [legendre_seven(v) for v in gll_nodes]
    weights = [2.0 / (degree * (degree + 1) * v * v) for v in end_values]
    derivative = [[0.0] * 8 for _ in range(8)]
    for a in range(8):
        for b in range(8):
            if a != b:
                derivative[a][b] = end_values[a] / (end_values[b] * (gll_nodes[a] - gll_nodes[b]))
    derivative[0][0] = -degree * (degree + 1) / 4.0
    derivative[7][7] = degree * (degree + 1) / 4.0
    return (gll_nodes, weights, derivative)


NODES, WEIGHTS, DERIV = gll_tables()
DERIV_T = [[DERIV[b][a] for b in range(8)] for a in range(8)]


def split_two(x):
    hi = x.astype(bf16)
    lo = (x - hi.astype(f32)).astype(bf16)
    return hi, lo


def block_matrix(table):
    full = np.kron(np.eye(16), np.asarray(table, np.float64)).astype(np.float32)
    hi = full.astype(jnp.bfloat16)
    lo = (full - hi.astype(np.float32)).astype(jnp.bfloat16)
    return np.concatenate([hi, lo, hi], axis=1)


def apply_table(table, pieces):
    even = [pieces[b] + pieces[7 - b] for b in range(4)]
    odd = [pieces[b] - pieces[7 - b] for b in range(4)]
    outs = [None] * 8
    for a in range(4):
        s = None
        d = None
        for b in range(4):
            cs = 0.5 * (table[a][b] - table[a][7 - b])
            cd = 0.5 * (table[a][b] + table[a][7 - b])
            s = cs * odd[b] if s is None else s + cs * odd[b]
            d = cd * even[b] if d is None else d + cd * even[b]
        outs[a] = d + s
        outs[7 - a] = s - d
    return outs


def dot_nn(a, b):
    return lax.dot_general(a, b, (((1,), (0,)), ((), ())), preferred_element_type=f32)


def dot_nt(a, b):
    return lax.dot_general(a, b, (((1,), (1,)), ((), ())), preferred_element_type=f32)


def one_hot_rows(row, count, dtype=bf16):
    ids = lax.broadcasted_iota(jnp.int16, (count, row.shape[-1]), 0)
    return jnp.where(ids == row.astype(jnp.int16), jnp.ones((), dtype), jnp.zeros((), dtype))


def weight_rows():
    k = lax.broadcasted_iota(i32, (8, 128), 0)
    out = jnp.zeros((8, 128), f32)
    for j in range(8):
        out = jnp.where(k == j, WEIGHTS[j], out)
    return out


def start_copies(pairs, sems):
    copies = [pltpu.make_async_copy(src, dst, sems.at[n]) for n, (src, dst) in enumerate(pairs)]
    for copy in copies:
        copy.start()
    return copies


def query_kernel(owner_any, donor_any, coords_any, payload_ref, rank_any, owner_ref, donor_ref, coords_ref, rank_ref, sems):
    copies = start_copies(
        [(owner_any, owner_ref), (donor_any, donor_ref), (coords_any, coords_ref)], sems
    )
    copies[0].wait()
    rows = owner_ref.shape[1]
    half = rows // 2
    owner = owner_ref[...]
    step = 256
    before = (
        lax.broadcasted_iota(i32, (step, step), 0) < lax.broadcasted_iota(i32, (step, step), 1)
    )
    before = jnp.where(before, 1.0, 0.0).astype(bf16)
    total = jnp.zeros((128, 1), f32)
    hots = []
    ranks = []
    for c in range(rows // step):
        sl = slice(c * step, (c + 1) * step)
        oh = one_hot_rows(owner[:, sl], 128)
        ohf = oh.astype(f32)
        cum = dot_nn(oh, before) + total
        total = total + jnp.sum(ohf, axis=1, keepdims=True)
        rank = jnp.sum(cum * ohf, axis=0, keepdims=True).astype(i32)
        rank_ref[:, sl] = rank
        hots.append(oh)
        ranks.append(rank)
    out = pltpu.make_async_copy(rank_ref, rank_any, sems.at[3])
    out.start()
    copies[1].wait()
    copies[2].wait()
    acc = [jnp.zeros((128, 128), f32) for _ in range(3)]
    for c in range(rows // step):
        sl = slice(c * step, (c + 1) * step)
        pick = lax.broadcasted_iota(i32, (32, step), 0) == ranks[c]
        col = lax.broadcasted_iota(i32, (1, step), 1) + c * step
        ident = (jnp.where(col < half, 128, 0) + donor_ref[:, sl]).astype(f32)
        parts = [[], [], []]
        for v in range(3):
            x = coords_ref[v : v + 1, sl]
            hi = x.astype(bf16).astype(f32)
            rest = x - hi
            mid = rest.astype(bf16).astype(f32)
            for p, val in enumerate((hi, mid, rest - mid)):
                parts[p].append(jnp.where(pick, val, 0.0).astype(bf16))
        zero = jnp.zeros((32, step), bf16)
        parts[0].append(jnp.where(pick, ident, 0.0).astype(bf16))
        parts[1].append(zero)
        parts[2].append(zero)
        for p in range(3):
            acc[p] = acc[p] + dot_nt(hots[c], jnp.concatenate(parts[p], axis=0))
    payload_ref[...] = acc[0] + (acc[1] + acc[2])
    out.wait()


def prepare_kernel(flags_ref, owner_any, rank_any, point_any, load_any, inv_any, table_any, mask_any, low_any, high_any,
                   load_ref, inv_ref, table_ref, mask_ref, low_ref, high_ref, sems):
    copies = start_copies(
        [(owner_any, table_ref.at[0:1]), (rank_any, table_ref.at[1:2]), (point_any, table_ref.at[2:3])], sems
    )
    for n in range(5):
        mask_ref[n] = jnp.full((8, 128), flags_ref[n], i32).astype(f32)
    for copy in copies:
        copy.wait()
    for n, ref in enumerate((low_ref, high_ref)):
        ref[0:2, :] = table_ref[0:2, :]
        ref[2:3, :] = (table_ref[2:3, :] + 1) * flags_ref[n + 2] - 1
    half = table_ref.shape[1] // 2
    wk = weight_rows()
    for m in range(2):
        point = table_ref[2:3, m * half : (m + 1) * half]
        q = lax.shift_right_logical(point, 7)
        e = lax.bitwise_and(point, 127)
        count = dot_nt(one_hot_rows(q, 512), one_hot_rows(e, 128))
        for ij in range(64):
            c = penalty_rate * volume_factor * WEIGHTS[ij // 8] * WEIGHTS[ij % 8]
            load_ref[m, ij * 8 : ij * 8 + 8, :] = (c * wk) * count[ij * 8 : ij * 8 + 8, :]
    k = lax.broadcasted_iota(i32, (8, 128), 0)
    e = lax.broadcasted_iota(i32, (8, 128), 1)
    shared = ((k == 0) & (e > 0)) | ((k == 7) & (e < 127))
    base = time_step / (volume_factor * wk * jnp.where(shared, 2.0, 1.0))
    for ij in range(64):
        i, j = ij // 8, ij % 8
        val = base * (1.0 / (WEIGHTS[i] * WEIGHTS[j]))
        if i in (0, 7):
            val = val * (1.0 - 0.5 * mask_ref[0 if i == 0 else 1])
        if j in (0, 7):
            val = val * (1.0 - 0.5 * mask_ref[2 if j == 0 else 3])
        inv_ref[ij * 8 : ij * 8 + 8, :] = val
    copies = start_copies(
        [(load_ref, load_any), (inv_ref, inv_any), (table_ref, table_any), (mask_ref, mask_any),
         (low_ref, low_any), (high_ref, high_any)],
        sems,
    )
    for copy in copies:
        copy.wait()


def relay_kernel(flags_ref, own_ref, below_ref, above_ref, low_ref, high_ref):
    for there, ref in ((flags_ref[0], low_ref), (flags_ref[1], high_ref)):
        for t, src in enumerate((own_ref, below_ref, above_ref)):
            ref[3 * t : 3 * t + 2, :] = src[0:2, :]
            ref[3 * t + 2 : 3 * t + 3, :] = (src[2:3, :] + 1) * there - 1


GHOSTS = [(-1, 0), (1, 0), (0, -1), (0, 1), (-1, -1), (-1, 1), (1, -1), (1, 1)]


def ghost_kernel(xp_ref, xn_ref, yp_ref, yn_ref, out_ref, out_any, sems):
    def write(n, src, base, side_x, side_y):
        point = src[base + 2 : base + 3, :]
        q = lax.shift_right_arithmetic(point, 7)
        i = lax.shift_right_arithmetic(q, 6)
        j = lax.bitwise_and(lax.shift_right_arithmetic(q, 3), 7)
        k = lax.bitwise_and(q, 7)
        good = point >= 0
        row = k
        if side_x is not None:
            good = good & (i == side_x)
        else:
            row = i * 8 + k
        if side_y is not None:
            good = good & (j == side_y)
        else:
            row = j * 8 + k
        out_ref[n, 0:2, :] = src[base : base + 2, :]
        out_ref[n, 2:3, :] = jnp.where(good, row, -1)
        out_ref[n, 3:4, :] = lax.bitwise_and(point, 127)

    write(2, yp_ref, 0, None, 7)
    write(3, yn_ref, 0, None, 0)
    for src, below in ((xp_ref, 1), (xn_ref, 0)):
        for base, side_y, low, high in ((0, None, 0, 1), (3, 7, 4, 6), (6, 0, 5, 7)):
            write(below * low + (1 - below) * high, src, base, 7 * below, side_y)
    copies = start_copies([(out_ref, out_any)], sems)
    copies[0].wait()


def local_rates(u_ref, vel_ref, nu_ref, load_ref, deep_ref, out_ref, ax_ref, ay_ref, fz_ref, copies):
    wk = weight_rows()

    def depth(table, pick):
        chunks = []
        for c in range(4):
            rows = slice(c * 128, (c + 1) * 128)
            hi, lo = split_two(jnp.concatenate([pick(0, rows), pick(1, rows)], axis=1))
            chunks.append(dot_nn(table, jnp.concatenate([hi, hi, lo], axis=0)))
        return chunks

    az = depth(deep_ref[0], lambda m, rows: u_ref[m, rows, :])
    for m in range(2):
        for j in range(8):
            outs = apply_table(DERIV, [u_ref[m, i * 64 + j * 8 : i * 64 + j * 8 + 8, :] for i in range(8)])
            for i in range(8):
                ax_ref[m, i * 64 + j * 8 : i * 64 + j * 8 + 8, :] = outs[i]
    for copy in copies:
        copy.wait()
    for m in range(2):
        wnu = 4.0 * volume_factor * wk * nu_ref[m : m + 1, :]
        wad = 2.0 * volume_factor * wk
        for i in range(8):
            outs = apply_table(DERIV, [u_ref[m, i * 64 + j * 8 : i * 64 + j * 8 + 8, :] for j in range(8)])
            fluxes = []
            for j in range(8):
                ij = i * 8 + j
                rows = slice(ij * 8, ij * 8 + 8)
                c = WEIGHTS[i] * WEIGHTS[j]
                gx = ax_ref[m, rows, :]
                gy = outs[j]
                gz = az[ij // 16][(ij % 16) * 8 : (ij % 16) * 8 + 8, m * 128 : (m + 1) * 128]
                adv = vel_ref[0, m, rows, :] * gx + vel_ref[1, m, rows, :] * gy + vel_ref[2, m, rows, :] * gz
                out_ref[m, rows, :] = -((c * wad) * adv) - load_ref[m, rows, :] * u_ref[m, rows, :]
                flux = c * wnu
                ax_ref[m, rows, :] = flux * gx
                fz_ref[m, rows, :] = flux * gz
                fluxes.append(flux * gy)
            outs = apply_table(DERIV_T, fluxes)
            for j in range(8):
                rows = slice(i * 64 + j * 8, i * 64 + j * 8 + 8)
                out_ref[m, rows, :] = out_ref[m, rows, :] - outs[j]
    bz = depth(deep_ref[1], lambda m, rows: fz_ref[m, rows, :])
    for m in range(2):
        for j in range(8):
            outs = apply_table(DERIV_T, [ax_ref[m, i * 64 + j * 8 : i * 64 + j * 8 + 8, :] for i in range(8)])
            for i in range(8):
                ij = i * 8 + j
                rows = slice(ij * 8, ij * 8 + 8)
                gz = bz[ij // 16][(ij % 16) * 8 : (ij % 16) * 8 + 8, m * 128 : (m + 1) * 128]
                out_ref[m, rows, :] = (out_ref[m, rows, :] - outs[i]) - gz


def send_faces(loc_ref, mask_ref, xl_ref, xr_ref, yl_ref, yr_ref, keep_ref):
    odd = mask_ref[4] > 0.5
    for m in range(2):
        for n in range(8):
            rows = slice(n * 8, n * 8 + 8)
            low = loc_ref[m, rows, :] * mask_ref[0]
            high = loc_ref[m, 448 + n * 8 : 456 + n * 8, :] * mask_ref[1]
            xl_ref[m, rows, :] = jnp.where(odd, low, high)
            xr_ref[m, rows, :] = jnp.where(odd, high, low)
            yl_ref[m, rows, :] = loc_ref[m, n * 64 : n * 64 + 8, :]
            yr_ref[m, rows, :] = loc_ref[m, n * 64 + 56 : n * 64 + 64, :]
    keep_ref[0:2] = mask_ref[2:4]
    keep_ref[2] = mask_ref[4]


def send_first_faces(loc_ref, mask_ref, xl_ref, xr_ref, yl_ref, yr_ref, keep_ref):
    for m in range(2):
        for n in range(8):
            rows = slice(n * 8, n * 8 + 8)
            xl_ref[m, rows, :] = loc_ref[m, rows, :]
            xr_ref[m, rows, :] = loc_ref[m, 448 + n * 8 : 456 + n * 8, :]
            yl_ref[m, rows, :] = loc_ref[m, n * 64 : n * 64 + 8, :] * mask_ref[2]
            yr_ref[m, rows, :] = loc_ref[m, n * 64 + 56 : n * 64 + 64, :] * mask_ref[3]
    keep_ref[0:2] = mask_ref[0:2]
    keep_ref[2] = mask_ref[4]


def first_edge_kernel(xl_ref, xr_ref, yn_ref, yp_ref, keep_ref, xl_out, xr_out):
    for m in range(2):
        for src, dst, i in ((xl_ref, xl_out, 0), (xr_ref, xr_out, 7)):
            mask = keep_ref[0 if i == 0 else 1]
            for j in range(8):
                val = src[m, j * 8 : j * 8 + 8, :]
                if j == 0:
                    val = val + yp_ref[m, i * 8 : i * 8 + 8, :]
                if j == 7:
                    val = val + yn_ref[m, i * 8 : i * 8 + 8, :]
                dst[m, j * 8 : j * 8 + 8, :] = val * mask


def local_kernel(u_any, vel_any, nu_any, load_any, deep_any, mask_any, loc_ref, xl_ref, xr_ref, yl_ref, yr_ref, keep_ref,
                 u_ref, vel_ref, nu_ref, load_ref, deep_ref, mask_ref, ax_ref, ay_ref, fz_ref, sems):
    copies = start_copies(
        [(u_any, u_ref), (deep_any, deep_ref), (nu_any, nu_ref), (vel_any, vel_ref), (load_any, load_ref),
         (mask_any, mask_ref)],
        sems,
    )
    copies[0].wait()
    copies[1].wait()
    local_rates(u_ref, vel_ref, nu_ref, load_ref, deep_ref, loc_ref, ax_ref, ay_ref, fz_ref, copies[2:])
    send_first_faces(loc_ref, mask_ref, xl_ref, xr_ref, yl_ref, yr_ref, keep_ref)


def interpolate(u, received_ref, ans_ref, wx_ref, wy_ref, wz_ref):
    parts = [split_two(v) for v in u]
    cat = jnp.concatenate([parts[0][0], parts[1][0], parts[0][1], parts[1][1]], axis=1)
    turned = received_ref[...].T
    for v, ref in enumerate((wx_ref, wy_ref, wz_ref)):
        x = turned[v * 32 : v * 32 + 32, :]
        diff = [x - NODES[m] for m in range(8)]
        pre = [None] * 8
        suf = [None] * 8
        for m in range(1, 8):
            pre[m] = diff[m - 1] if pre[m - 1] is None else pre[m - 1] * diff[m - 1]
        for m in range(6, -1, -1):
            suf[m] = diff[m + 1] if suf[m + 1] is None else suf[m + 1] * diff[m + 1]
        for j in range(8):
            c = 1.0
            for m in range(8):
                if m != j:
                    c = c / (NODES[j] - NODES[m])
            w = suf[j] if pre[j] is None else (pre[j] if suf[j] is None else pre[j] * suf[j])
            w = w * c
            if ref is wz_ref:
                ref[:, j, :] = w
            else:
                ref[j] = w
    ids = turned[96:128, :].astype(i32)
    rows = []
    for g in range(16):
        hot = [one_hot_rows(ids[s : s + 1, :], 256) for s in (2 * g, 2 * g + 1)]
        hot = jnp.concatenate(hot, axis=1)
        got = dot_nn(cat, jnp.concatenate([hot, hot], axis=0))
        for b in range(2):
            s = 2 * g + b
            total = None
            for j in range(8):
                acc = None
                for i in range(8):
                    term = wx_ref[i, s : s + 1, :] * got[i * 64 + j * 8 : i * 64 + j * 8 + 8, b * 128 : (b + 1) * 128]
                    acc = term if acc is None else acc + term
                acc = acc * wy_ref[j, s : s + 1, :]
                total = acc if total is None else total + acc
            rows.append(jnp.sum(total * wz_ref[s], axis=0, keepdims=True))
    answers = jnp.concatenate(rows, axis=0)
    blocks = [answers]
    for dx, dy in GHOSTS:
        blocks.append(pltpu.roll(answers, (-(4 * dx + dy)) % 128, 1))
    for a in range(3):
        group = blocks[4 * a : 4 * a + 4]
        if len(group) < 4:
            group = group + [jnp.zeros((32 * (4 - len(group)), 128), f32)]
        ans_ref[:, a, :] = jnp.concatenate(group, axis=0).T
    ans_ref[:, 3, :] = jnp.zeros((128, 128), f32)


def answer_kernel(u_ref, received_ref, ans_ref, wx_ref, wy_ref, wz_ref):
    interpolate([u_ref[0], u_ref[1]], received_ref, ans_ref, wx_ref, wy_ref, wz_ref)


def first_kernel(u_any, received_ref, ans_ref, u_ref, wx_ref, wy_ref, wz_ref, sems):
    copies = start_copies([(u_any, u_ref)], sems)
    copies[0].wait()
    interpolate([u_ref[0], u_ref[1]], received_ref, ans_ref, wx_ref, wy_ref, wz_ref)


def edge_kernel(yl_ref, yr_ref, pair_ref, cross_ref, keep_ref, yl_out, yr_out):
    odd = keep_ref[2] > 0.5
    for m in range(2):
        for src, dst, j in ((yl_ref, yl_out, 0), (yr_ref, yr_out, 7)):
            mask = keep_ref[0 if j == 0 else 1]
            pair = pair_ref[m, j * 8 : j * 8 + 8, :]
            cross = cross_ref[m, j * 8 : j * 8 + 8, :]
            for i in range(8):
                val = src[m, i * 8 : i * 8 + 8, :]
                if i == 0:
                    val = val + jnp.where(odd, pair, cross)
                if i == 7:
                    val = val + jnp.where(odd, cross, pair)
                dst[m, i * 8 : i * 8 + 8, :] = val * mask


def bring_kernel(after_ref, table_any, ghost_any, received_any, table_ref, ghost_ref, received_ref, sems):
    copies = start_copies([(table_any, table_ref), (ghost_any, ghost_ref), (received_any, received_ref)], sems)
    for copy in copies:
        copy.wait()


def first_bring_kernel(after_ref, table_any, received_any, table_ref, received_ref, sems):
    copies = start_copies([(table_any, table_ref), (received_any, received_ref)], sems)
    for copy in copies:
        copy.wait()


def with_faces(parts, m, ij):
    loc_ref, pair_ref, cross_ref, yn_ref, yp_ref, keep_ref, ring = parts
    i, j = ij // 8, ij % 8
    val = loc_ref[m, ij * 8 : ij * 8 + 8, :]
    if j == 0:
        val = val + yp_ref[m, i * 8 : i * 8 + 8, :]
    elif j == 7:
        val = val + yn_ref[m, i * 8 : i * 8 + 8, :]
    if ring and i in (0, 7):
        val = val + (cross_ref if i == 0 else pair_ref)[m, j * 8 : j * 8 + 8, :]
    elif i in (0, 7):
        pair = pair_ref[m, j * 8 : j * 8 + 8, :]
        cross = cross_ref[m, j * 8 : j * 8 + 8, :]
        odd = keep_ref[2] > 0.5
        val = val + (jnp.where(odd, pair, cross) if i == 0 else jnp.where(odd, cross, pair))
    return val


def picked(block, owner, rank):
    parts = []
    for c in range(owner.shape[1] // 128):
        sl = slice(c * 128, (c + 1) * 128)
        index = jnp.broadcast_to(owner[:, sl], (32, 128))
        got = jnp.take_along_axis(block, index, axis=1, mode="promise_in_bounds")
        pick = lax.broadcasted_iota(i32, (32, 128), 0) == rank[:, sl]
        parts.append(jnp.sum(jnp.where(pick, got, 0.0), axis=0, keepdims=True))
    g = jnp.concatenate(parts, axis=1)
    return split_two(g)


def placed(row, count, hi, lo):
    at = lax.broadcasted_iota(jnp.int16, (count, row.shape[-1]), 0) == row.astype(jnp.int16)
    zero = jnp.zeros((), bf16)
    return jnp.concatenate([jnp.where(at, hi, zero), jnp.where(at, lo, zero)], axis=0)


def add_replies(replies_ref, table_ref, ghost_ref, parts, work_ref):
    half = table_ref.shape[1] // 2
    wk = weight_rows()
    blocks = []
    for a in range(3):
        turned = replies_ref[:, a, :].T
        for c in range(4):
            if 4 * a + c < 9:
                blocks.append(turned[c * 32 : c * 32 + 32, :])
    for m in range(2):
        sl = slice(m * half, (m + 1) * half)
        faces = {}
        for n, where in enumerate(GHOSTS):
            ghi, glo = picked(blocks[n + 1], ghost_ref[n, 0:1, sl], ghost_ref[n, 1:2, sl])
            size = 8 if where[0] and where[1] else 64
            lhs = placed(ghost_ref[n, 2:3, sl], size, ghi, glo)
            both = dot_nt(lhs, one_hot_rows(ghost_ref[n, 3:4, sl], 128))
            faces[where] = both[0:size, :] + both[size : 2 * size, :]
        ghi, glo = picked(blocks[0], table_ref[0:1, sl], table_ref[1:2, sl])
        point = table_ref[2:3, sl]
        q = lax.shift_right_logical(point, 7)
        e = lax.bitwise_and(point, 127)
        both = dot_nt(one_hot_rows(q, 512), placed(e, 128, ghi, glo))
        summed = both[:, 0:128] + both[:, 128:256]
        for ij in range(64):
            rows = slice(ij * 8, ij * 8 + 8)
            i, j = ij // 8, ij % 8
            dx = {0: -1, 7: 1}.get(i, 0)
            dy = {0: -1, 7: 1}.get(j, 0)
            c = penalty_rate * volume_factor * WEIGHTS[i] * WEIGHTS[j]
            g = summed[rows, :]
            if dx:
                g = g + faces[(dx, 0)][j * 8 : j * 8 + 8, :]
            if dy:
                g = g + faces[(0, dy)][i * 8 : i * 8 + 8, :]
            if dx and dy:
                g = g + faces[(dx, dy)]
            work_ref[m, rows, :] = with_faces(parts, m, ij) + (c * wk) * g


def advance(blend, start_ref, u_ref, inv_ref, work_ref, new_ref):
    lane = lax.broadcasted_iota(i32, (64, 128), 1)
    for m in range(2):
        left = work_ref[m, pl.ds(0, 64, stride=8), :]
        right = work_ref[m, pl.ds(7, 64, stride=8), :]
        work_ref[m, pl.ds(0, 64, stride=8), :] = left + jnp.where(lane > 0, pltpu.roll(right, 1, 1), 0.0)
        work_ref[m, pl.ds(7, 64, stride=8), :] = right + jnp.where(lane < 127, pltpu.roll(left, 127, 1), 0.0)
        new = u_ref[m] + inv_ref[...] * work_ref[m]
        if blend is not None:
            new = blend[0] * start_ref[m] + blend[1] * new
        new_ref[m] = new


def step_kernel(blend, replies_ref, table_ref, ghost_ref, old_ref, xn_ref, xp_ref, yn_ref, yp_ref, kept_ref, start_any, u_any, inv_any, vel_any, nu_any, load_any,
                deep_any, mask_any, new_any, new_ref, loc_ref, xl_ref, xr_ref, yl_ref, yr_ref, keep_ref,
                work_ref, start_ref, u_ref, inv_ref, vel_ref, nu_ref, load_ref, deep_ref, mask_ref,
                ax_ref, ay_ref, fz_ref, sems):
    copies = start_copies(
        [(u_any, u_ref), (inv_any, inv_ref), (start_any, start_ref), (deep_any, deep_ref), (nu_any, nu_ref),
         (vel_any, vel_ref), (load_any, load_ref), (mask_any, mask_ref)],
        sems,
    )
    add_replies(replies_ref, table_ref, ghost_ref, (old_ref, xn_ref, xp_ref, yn_ref, yp_ref, kept_ref, blend is None), work_ref)
    for copy in copies[:4]:
        copy.wait()
    advance(blend, start_ref, u_ref, inv_ref, work_ref, new_ref)
    out = pltpu.make_async_copy(new_ref, new_any, sems.at[8])
    out.start()
    local_rates(new_ref, vel_ref, nu_ref, load_ref, deep_ref, loc_ref, ax_ref, ay_ref, fz_ref, copies[4:])
    send_faces(loc_ref, mask_ref, xl_ref, xr_ref, yl_ref, yr_ref, keep_ref)
    out.wait()


def last_kernel(blend, replies_ref, table_ref, ghost_ref, old_ref, xn_ref, xp_ref, yn_ref, yp_ref, kept_ref, start_any, u_any, inv_any, new_ref,
                work_ref, start_ref, u_ref, inv_ref, sems):
    copies = start_copies([(u_any, u_ref), (inv_any, inv_ref), (start_any, start_ref)], sems)
    add_replies(replies_ref, table_ref, ghost_ref, (old_ref, xn_ref, xp_ref, yn_ref, yp_ref, kept_ref, blend is None), work_ref)
    for copy in copies:
        copy.wait()
    advance(blend, start_ref, u_ref, inv_ref, work_ref, new_ref)


PINNED = "ap"
SPACES = {"p": pltpu.VMEM, "v": pltpu.VMEM, "a": pltpu.HBM, "s": pltpu.SMEM}


def call(kernel, outs, ins, scratch=(), spaces="", out_spaces=""):
    return pl.pallas_call(
        kernel,
        out_shape=[SPACES[c](s, d) if c in PINNED else jax.ShapeDtypeStruct(s, d) for (s, d), c in zip(outs, out_spaces)],
        in_specs=[pl.BlockSpec(memory_space=SPACES[c]) for c in spaces],
        out_specs=[pl.BlockSpec(memory_space=SPACES[c]) for c in out_spaces],
        scratch_shapes=list(scratch),
        compiler_params=pltpu.CompilerParams(vmem_limit_bytes=28 << 20),
    )(*[pltpu.with_memory_space_constraint(x, SPACES[c]) if c in PINNED else x for x, c in zip(ins, spaces)])


def passed_around(value, axis, steps):
    count = lax.axis_size(axis)
    return lax.ppermute(value, axis, [(n, (n + steps) % count) for n in range(count)])


def swapped(pair, cross):
    count = lax.axis_size("gx")
    across = [min(max(((n + 1) ^ 1) - 1, 0), count - 1) for n in range(count)]
    return (
        lax.ppermute(pair, "gx", [(n, n ^ 1) for n in range(count)]),
        lax.ppermute(cross, "gx", [(n, across[n]) for n in range(count)]),
    )


def exchange(x):
    return lax.all_to_all(x, ("gx", "gy"), split_axis=0, concat_axis=0, tiled=True)


def body(scalar, velocity, diffusivity, recv_owner, donor_elem, recv_point, recv_coords):
    rows = recv_owner.shape[0]
    field = (2, 512, 128)
    face = (2, 64, 128)
    start = scalar.reshape(field)
    flow = velocity.reshape((3,) + field)
    nu = diffusivity.reshape(2, 128)
    owner = recv_owner.reshape(1, rows)
    donor = donor_elem.reshape(1, rows)
    point = recv_point.reshape(1, rows)
    deep = jnp.asarray(np.stack([block_matrix(DERIV), block_matrix(DERIV_T)]))

    def vmem(shape, dtype=f32):
        return pltpu.VMEM(shape, dtype)

    def dma(count):
        return pltpu.SemaphoreType.DMA((count,))

    line = vmem((1, rows), i32)
    weights_scratch = [vmem((8, 32, 128)), vmem((8, 32, 128)), vmem((32, 8, 128))]
    local_scratch = [vmem((3,) + field), vmem((2, 128)), vmem(field), vmem((2, 128, 384), bf16), vmem((5, 8, 128))]
    local_scratch = local_scratch + [vmem(field)] * 3
    tables = [((3, rows), i32)] * 2

    payload, rank = call(
        query_kernel,
        [((128, 128), f32), ((1, rows), i32)],
        (owner, donor, recv_coords),
        [line, line, vmem((3, rows)), line, dma(4)],
        "aaa",
        "va",
    )
    received = exchange(payload)

    ix, iy = lax.axis_index("gx"), lax.axis_index("gy")
    inside = [ix > 0, ix < lax.axis_size("gx") - 1, iy > 0, iy < lax.axis_size("gy") - 1]
    flags = jnp.stack(inside + [ix % 2 == 1]).astype(i32)
    load, inv, table, mask, low, high = call(
        prepare_kernel,
        [(field, f32), ((512, 128), f32), ((3, rows), i32), ((5, 8, 128), f32)] + tables,
        (flags, owner, rank, point),
        [vmem(field), vmem((512, 128)), vmem((3, rows), i32), vmem((5, 8, 128))]
        + [vmem((3, rows), i32)] * 2
        + [dma(6)],
        "saaa",
        "aaaaaa",
    )

    def along_y(yl, yr):
        return passed_around(yl, "gy", -1), passed_around(yr, "gy", 1)

    def faces_along_y(yl, yr, xn, xp, keep):
        return along_y(*call(edge_kernel, [(face, f32)] * 2, (yl, yr, xn, xp, keep), (), "vvvvv", "vv"))

    def bring(after):
        return call(
            bring_kernel,
            [((3, rows), i32), ((8, 4, rows), i32), ((128, 128), f32)],
            (after, table, ghosts, received),
            [dma(3)],
            "vaaa",
            "vvv",
        )

    outs = [(field, f32)] + [(face, f32)] * 4 + [((3, 8, 128), f32)]
    u = start
    loc, xl, xr, yl, yr, keep = call(
        local_kernel,
        outs,
        (u, flow, nu, load, deep, mask),
        [vmem(field)] + local_scratch + [dma(6)],
        "aaaaaa",
        "vvvvvv",
    )
    received, loc, yl, yr, low, high = lax.optimization_barrier((received, loc, yl, yr, low, high))
    yn, yp = along_y(yl, yr)
    table_n, table_p = along_y(low, high)
    answers = call(
        first_kernel,
        [((128, 4, 128), f32)],
        (u, received),
        [vmem(field)] + weights_scratch + [dma(1)],
        "av",
        "p",
    )[0]
    answers, yn, yp, table_n, table_p = lax.optimization_barrier((answers, yn, yp, table_n, table_p))
    replies = exchange(answers)
    xl, xr = call(first_edge_kernel, [(face, f32)] * 2, (xl, xr, yn, yp, keep), (), "vvvvv", "vv")
    xn, xp = passed_around(xl, "gx", -1), passed_around(xr, "gx", 1)
    low, high = call(
        relay_kernel, [((9, rows), i32)] * 2, (flags, table, table_p, table_n), (), "svvv", "vv"
    )
    tables_n, tables_p = passed_around(low, "gx", -1), passed_around(high, "gx", 1)
    near, ghosts = call(
        ghost_kernel,
        [((8, 4, rows), i32)] * 2,
        (tables_p, tables_n, table_p, table_n),
        [dma(1)],
        "vvvv",
        "va",
    )
    own, asked = call(
        first_bring_kernel,
        [((3, rows), i32), ((128, 128), f32)],
        (table_n, table, received),
        [dma(2)],
        "vaa",
        "vv",
    )
    for blend in (None, (0.75, 0.25)):
        u, near_u, loc, xl, xr, yl, yr, keep = call(
            lambda *refs, blend=blend: step_kernel(blend, *refs),
            [(field, f32)] * 2 + outs,
            (replies, own, near, loc, xn, xp, yn, yp, keep, start, u, inv, flow, nu, load, deep, mask),
            [vmem(field)] * 3 + [vmem((512, 128))] + local_scratch + [dma(9)],
            "vvvvvvvvvaaaaaaaa",
            "avvvvvvv",
        )
        xn, xp = swapped(xl, xr)
        answers = call(
            answer_kernel,
            [((128, 4, 128), f32)],
            (near_u, asked),
            weights_scratch,
            "vv",
            "p",
        )[0]
        answers, xn, xp = lax.optimization_barrier((answers, xn, xp))
        replies = exchange(answers)
        yn, yp = faces_along_y(yl, yr, xn, xp, keep)
        own, near, asked = bring(keep)
    third = call(
        lambda *refs: last_kernel((1.0 / 3.0, 2.0 / 3.0), *refs),
        [(field, f32)],
        (replies, own, near, loc, xn, xp, yn, yp, keep, start, u, inv),
        [vmem(field)] * 3 + [vmem((512, 128)), dma(3)],
        "vvvvvvvvvaaa",
        "v",
    )[0]
    return third.reshape(scalar.shape)


def solution(mesh):
    return jax.shard_map(
        body,
        mesh=mesh,
        in_specs=(
            P(None, None, "gx", "gy", None),
            P(None, None, None, "gx", "gy", None),
            P(None, "gx", "gy", None),
            P(("gx", "gy"), None),
            P(("gx", "gy")),
            P(("gx", "gy")),
            P(None, ("gx", "gy")),
        ),
        out_specs=P(None, None, "gx", "gy", None),
        check_vma=False,
    )
```

```python
import jax
import jax.numpy as jnp
import numpy as np
from jax import lax
from jax.experimental import pallas as pl
from jax.experimental.pallas import tpu as pltpu
from jax.sharding import PartitionSpec as P

time_step = 0.01
penalty_rate = 50.0
metric = 2.0
volume_factor = 0.125
node_inner = [0.8717401485096066, 0.5917001814331423, 0.20929921790247888]
f32 = jnp.float32
bf16 = jnp.bfloat16
i32 = jnp.int32


def legendre_seven(point):
    before, current = (1.0, point)
    for order in range(1, 7):
        before, current = (
            current,
            ((2 * order + 1) * point * current - order * before) / (order + 1),
        )
    return current


def gll_tables():
    degree = 7
    gll_nodes = [-1.0] + [-v for v in node_inner] + node_inner[::-1] + [1.0]
    end_values = [legendre_seven(v) for v in gll_nodes]
    weights = [2.0 / (degree * (degree + 1) * v * v) for v in end_values]
    derivative = [[0.0] * 8 for _ in range(8)]
    for a in range(8):
        for b in range(8):
            if a != b:
                derivative[a][b] = end_values[a] / (end_values[b] * (gll_nodes[a] - gll_nodes[b]))
    derivative[0][0] = -degree * (degree + 1) / 4.0
    derivative[7][7] = degree * (degree + 1) / 4.0
    return (gll_nodes, weights, derivative)


NODES, WEIGHTS, DERIV = gll_tables()
DERIV_T = [[DERIV[b][a] for b in range(8)] for a in range(8)]


def split_two(x):
    hi = x.astype(bf16)
    lo = (x - hi.astype(f32)).astype(bf16)
    return hi, lo


def block_matrix(table):
    full = np.kron(np.eye(16), np.asarray(table, np.float64)).astype(np.float32)
    hi = full.astype(jnp.bfloat16)
    lo = (full - hi.astype(np.float32)).astype(jnp.bfloat16)
    return np.concatenate([hi, lo, hi], axis=1)


def apply_table(table, pieces):
    even = [pieces[b] + pieces[7 - b] for b in range(4)]
    odd = [pieces[b] - pieces[7 - b] for b in range(4)]
    outs = [None] * 8
    for a in range(4):
        s = None
        d = None
        for b in range(4):
            cs = 0.5 * (table[a][b] - table[a][7 - b])
            cd = 0.5 * (table[a][b] + table[a][7 - b])
            s = cs * odd[b] if s is None else s + cs * odd[b]
            d = cd * even[b] if d is None else d + cd * even[b]
        outs[a] = d + s
        outs[7 - a] = s - d
    return outs


def dot_nn(a, b):
    return lax.dot_general(a, b, (((1,), (0,)), ((), ())), preferred_element_type=f32)


def dot_nt(a, b):
    return lax.dot_general(a, b, (((1,), (1,)), ((), ())), preferred_element_type=f32)


def one_hot_rows(row, count, dtype=bf16):
    ids = lax.broadcasted_iota(jnp.int16, (count, row.shape[-1]), 0)
    return jnp.where(ids == row.astype(jnp.int16), jnp.ones((), dtype), jnp.zeros((), dtype))


def weight_rows():
    k = lax.broadcasted_iota(i32, (8, 128), 0)
    out = jnp.zeros((8, 128), f32)
    for j in range(8):
        out = jnp.where(k == j, WEIGHTS[j], out)
    return out


def start_copies(pairs, sems):
    copies = [pltpu.make_async_copy(src, dst, sems.at[n]) for n, (src, dst) in enumerate(pairs)]
    for copy in copies:
        copy.start()
    return copies


def query_kernel(owner_any, donor_any, coords_any, payload_ref, rank_any, owner_ref, donor_ref, coords_ref, rank_ref, sems):
    copies = start_copies(
        [(owner_any, owner_ref), (donor_any, donor_ref), (coords_any, coords_ref)], sems
    )
    copies[0].wait()
    rows = owner_ref.shape[1]
    half = rows // 2
    owner = owner_ref[...]
    step = 256
    before = (
        lax.broadcasted_iota(i32, (step, step), 0) < lax.broadcasted_iota(i32, (step, step), 1)
    )
    before = jnp.where(before, 1.0, 0.0).astype(bf16)
    total = jnp.zeros((128, 1), f32)
    hots = []
    ranks = []
    for c in range(rows // step):
        sl = slice(c * step, (c + 1) * step)
        oh = one_hot_rows(owner[:, sl], 128)
        ohf = oh.astype(f32)
        cum = dot_nn(oh, before) + total
        total = total + jnp.sum(ohf, axis=1, keepdims=True)
        rank = jnp.sum(cum * ohf, axis=0, keepdims=True).astype(i32)
        rank_ref[:, sl] = rank
        hots.append(oh)
        ranks.append(rank)
    out = pltpu.make_async_copy(rank_ref, rank_any, sems.at[3])
    out.start()
    copies[1].wait()
    copies[2].wait()
    acc = [jnp.zeros((128, 128), f32) for _ in range(3)]
    for c in range(rows // step):
        sl = slice(c * step, (c + 1) * step)
        pick = lax.broadcasted_iota(i32, (32, step), 0) == ranks[c]
        col = lax.broadcasted_iota(i32, (1, step), 1) + c * step
        ident = (jnp.where(col < half, 128, 0) + donor_ref[:, sl]).astype(f32)
        parts = [[], [], []]
        for v in range(3):
            x = coords_ref[v : v + 1, sl]
            hi = x.astype(bf16).astype(f32)
            rest = x - hi
            mid = rest.astype(bf16).astype(f32)
            for p, val in enumerate((hi, mid, rest - mid)):
                parts[p].append(jnp.where(pick, val, 0.0).astype(bf16))
        zero = jnp.zeros((32, step), bf16)
        parts[0].append(jnp.where(pick, ident, 0.0).astype(bf16))
        parts[1].append(zero)
        parts[2].append(zero)
        for p in range(3):
            acc[p] = acc[p] + dot_nt(hots[c], jnp.concatenate(parts[p], axis=0))
    payload_ref[...] = acc[0] + (acc[1] + acc[2])
    out.wait()


def prepare_kernel(flags_ref, owner_any, rank_any, point_any, load_any, inv_any, table_any, mask_any, low_any, high_any,
                   load_ref, inv_ref, table_ref, mask_ref, low_ref, high_ref, sems):
    copies = start_copies(
        [(owner_any, table_ref.at[0:1]), (rank_any, table_ref.at[1:2]), (point_any, table_ref.at[2:3])], sems
    )
    for n in range(5):
        mask_ref[n] = jnp.full((8, 128), flags_ref[n], i32).astype(f32)
    for copy in copies:
        copy.wait()
    for n, ref in enumerate((low_ref, high_ref)):
        ref[0:2, :] = table_ref[0:2, :]
        ref[2:3, :] = (table_ref[2:3, :] + 1) * flags_ref[n + 2] - 1
    half = table_ref.shape[1] // 2
    wk = weight_rows()
    for m in range(2):
        point = table_ref[2:3, m * half : (m + 1) * half]
        q = lax.shift_right_logical(point, 7)
        e = lax.bitwise_and(point, 127)
        count = dot_nt(one_hot_rows(q, 512), one_hot_rows(e, 128))
        for ij in range(64):
            c = penalty_rate * volume_factor * WEIGHTS[ij // 8] * WEIGHTS[ij % 8]
            load_ref[m, ij * 8 : ij * 8 + 8, :] = (c * wk) * count[ij * 8 : ij * 8 + 8, :]
    k = lax.broadcasted_iota(i32, (8, 128), 0)
    e = lax.broadcasted_iota(i32, (8, 128), 1)
    shared = ((k == 0) & (e > 0)) | ((k == 7) & (e < 127))
    base = time_step / (volume_factor * wk * jnp.where(shared, 2.0, 1.0))
    for ij in range(64):
        i, j = ij // 8, ij % 8
        val = base * (1.0 / (WEIGHTS[i] * WEIGHTS[j]))
        if i in (0, 7):
            val = val * (1.0 - 0.5 * mask_ref[0 if i == 0 else 1])
        if j in (0, 7):
            val = val * (1.0 - 0.5 * mask_ref[2 if j == 0 else 3])
        inv_ref[ij * 8 : ij * 8 + 8, :] = val
    copies = start_copies(
        [(load_ref, load_any), (inv_ref, inv_any), (table_ref, table_any), (mask_ref, mask_any),
         (low_ref, low_any), (high_ref, high_any)],
        sems,
    )
    for copy in copies:
        copy.wait()


def relay_kernel(flags_ref, own_ref, below_ref, above_ref, low_ref, high_ref):
    for there, ref in ((flags_ref[0], low_ref), (flags_ref[1], high_ref)):
        for t, src in enumerate((own_ref, below_ref, above_ref)):
            ref[3 * t : 3 * t + 2, :] = src[0:2, :]
            ref[3 * t + 2 : 3 * t + 3, :] = (src[2:3, :] + 1) * there - 1


GHOSTS = [(-1, 0), (1, 0), (0, -1), (0, 1), (-1, -1), (-1, 1), (1, -1), (1, 1)]


def ghost_kernel(xp_ref, xn_ref, yp_ref, yn_ref, out_ref, out_any, sems):
    def write(n, src, base, side_x, side_y):
        point = src[base + 2 : base + 3, :]
        q = lax.shift_right_arithmetic(point, 7)
        i = lax.shift_right_arithmetic(q, 6)
        j = lax.bitwise_and(lax.shift_right_arithmetic(q, 3), 7)
        k = lax.bitwise_and(q, 7)
        good = point >= 0
        row = k
        if side_x is not None:
            good = good & (i == side_x)
        else:
            row = i * 8 + k
        if side_y is not None:
            good = good & (j == side_y)
        else:
            row = j * 8 + k
        out_ref[n, 0:2, :] = src[base : base + 2, :]
        out_ref[n, 2:3, :] = jnp.where(good, row, -1)
        out_ref[n, 3:4, :] = lax.bitwise_and(point, 127)

    write(2, yp_ref, 0, None, 7)
    write(3, yn_ref, 0, None, 0)
    for src, below in ((xp_ref, 1), (xn_ref, 0)):
        for base, side_y, low, high in ((0, None, 0, 1), (3, 7, 4, 6), (6, 0, 5, 7)):
            write(below * low + (1 - below) * high, src, base, 7 * below, side_y)
    copies = start_copies([(out_ref, out_any)], sems)
    copies[0].wait()


def local_rates(u_ref, vel_ref, nu_ref, load_ref, deep_ref, out_ref, ax_ref, ay_ref, fz_ref, copies):
    wk = weight_rows()

    def depth(table, pick):
        chunks = []
        for c in range(4):
            rows = slice(c * 128, (c + 1) * 128)
            hi, lo = split_two(jnp.concatenate([pick(0, rows), pick(1, rows)], axis=1))
            chunks.append(dot_nn(table, jnp.concatenate([hi, hi, lo], axis=0)))
        return chunks

    az = depth(deep_ref[0], lambda m, rows: u_ref[m, rows, :])
    for m in range(2):
        for j in range(8):
            outs = apply_table(DERIV, [u_ref[m, i * 64 + j * 8 : i * 64 + j * 8 + 8, :] for i in range(8)])
            for i in range(8):
                ax_ref[m, i * 64 + j * 8 : i * 64 + j * 8 + 8, :] = outs[i]
    for copy in copies:
        copy.wait()
    for m in range(2):
        wnu = 4.0 * volume_factor * wk * nu_ref[m : m + 1, :]
        wad = 2.0 * volume_factor * wk
        for i in range(8):
            outs = apply_table(DERIV, [u_ref[m, i * 64 + j * 8 : i * 64 + j * 8 + 8, :] for j in range(8)])
            fluxes = []
            for j in range(8):
                ij = i * 8 + j
                rows = slice(ij * 8, ij * 8 + 8)
                c = WEIGHTS[i] * WEIGHTS[j]
                gx = ax_ref[m, rows, :]
                gy = outs[j]
                gz = az[ij // 16][(ij % 16) * 8 : (ij % 16) * 8 + 8, m * 128 : (m + 1) * 128]
                adv = vel_ref[0, m, rows, :] * gx + vel_ref[1, m, rows, :] * gy + vel_ref[2, m, rows, :] * gz
                out_ref[m, rows, :] = -((c * wad) * adv) - load_ref[m, rows, :] * u_ref[m, rows, :]
                flux = c * wnu
                ax_ref[m, rows, :] = flux * gx
                fz_ref[m, rows, :] = flux * gz
                fluxes.append(flux * gy)
            outs = apply_table(DERIV_T, fluxes)
            for j in range(8):
                rows = slice(i * 64 + j * 8, i * 64 + j * 8 + 8)
                out_ref[m, rows, :] = out_ref[m, rows, :] - outs[j]
    bz = depth(deep_ref[1], lambda m, rows: fz_ref[m, rows, :])
    for m in range(2):
        for j in range(8):
            outs = apply_table(DERIV_T, [ax_ref[m, i * 64 + j * 8 : i * 64 + j * 8 + 8, :] for i in range(8)])
            for i in range(8):
                ij = i * 8 + j
                rows = slice(ij * 8, ij * 8 + 8)
                gz = bz[ij // 16][(ij % 16) * 8 : (ij % 16) * 8 + 8, m * 128 : (m + 1) * 128]
                out_ref[m, rows, :] = (out_ref[m, rows, :] - outs[i]) - gz


def send_faces(loc_ref, mask_ref, xl_ref, xr_ref, yl_ref, yr_ref, keep_ref):
    odd = mask_ref[4] > 0.5
    for m in range(2):
        for n in range(8):
            rows = slice(n * 8, n * 8 + 8)
            low = loc_ref[m, rows, :] * mask_ref[0]
            high = loc_ref[m, 448 + n * 8 : 456 + n * 8, :] * mask_ref[1]
            xl_ref[m, rows, :] = jnp.where(odd, low, high)
            xr_ref[m, rows, :] = jnp.where(odd, high, low)
            yl_ref[m, rows, :] = loc_ref[m, n * 64 : n * 64 + 8, :]
            yr_ref[m, rows, :] = loc_ref[m, n * 64 + 56 : n * 64 + 64, :]
    keep_ref[0:2] = mask_ref[2:4]
    keep_ref[2] = mask_ref[4]


def send_first_faces(loc_ref, mask_ref, xl_ref, xr_ref, yl_ref, yr_ref, keep_ref):
    for m in range(2):
        for n in range(8):
            rows = slice(n * 8, n * 8 + 8)
            xl_ref[m, rows, :] = loc_ref[m, rows, :]
            xr_ref[m, rows, :] = loc_ref[m, 448 + n * 8 : 456 + n * 8, :]
            yl_ref[m, rows, :] = loc_ref[m, n * 64 : n * 64 + 8, :] * mask_ref[2]
            yr_ref[m, rows, :] = loc_ref[m, n * 64 + 56 : n * 64 + 64, :] * mask_ref[3]
    keep_ref[0:2] = mask_ref[0:2]
    keep_ref[2] = mask_ref[4]


def first_edge_kernel(xl_ref, xr_ref, yn_ref, yp_ref, keep_ref, xl_out, xr_out):
    for m in range(2):
        for src, dst, i in ((xl_ref, xl_out, 0), (xr_ref, xr_out, 7)):
            mask = keep_ref[0 if i == 0 else 1]
            for j in range(8):
                val = src[m, j * 8 : j * 8 + 8, :]
                if j == 0:
                    val = val + yp_ref[m, i * 8 : i * 8 + 8, :]
                if j == 7:
                    val = val + yn_ref[m, i * 8 : i * 8 + 8, :]
                dst[m, j * 8 : j * 8 + 8, :] = val * mask


def local_kernel(u_any, vel_any, nu_any, load_any, deep_any, mask_any, loc_ref, xl_ref, xr_ref, yl_ref, yr_ref, keep_ref,
                 u_ref, vel_ref, nu_ref, load_ref, deep_ref, mask_ref, ax_ref, ay_ref, fz_ref, sems):
    copies = start_copies(
        [(u_any, u_ref), (deep_any, deep_ref), (nu_any, nu_ref), (vel_any, vel_ref), (load_any, load_ref),
         (mask_any, mask_ref)],
        sems,
    )
    copies[0].wait()
    copies[1].wait()
    local_rates(u_ref, vel_ref, nu_ref, load_ref, deep_ref, loc_ref, ax_ref, ay_ref, fz_ref, copies[2:])
    send_first_faces(loc_ref, mask_ref, xl_ref, xr_ref, yl_ref, yr_ref, keep_ref)


def interpolate(u_ref, received_ref, ans_ref, wx_ref, wy_ref, wz_ref, copies):
    turned = received_ref[...].T
    for v, ref in enumerate((wx_ref, wy_ref, wz_ref)):
        x = turned[v * 32 : v * 32 + 32, :]
        diff = [x - NODES[m] for m in range(8)]
        pre = [None] * 8
        suf = [None] * 8
        for m in range(1, 8):
            pre[m] = diff[m - 1] if pre[m - 1] is None else pre[m - 1] * diff[m - 1]
        for m in range(6, -1, -1):
            suf[m] = diff[m + 1] if suf[m + 1] is None else suf[m + 1] * diff[m + 1]
        for j in range(8):
            c = 1.0
            for m in range(8):
                if m != j:
                    c = c / (NODES[j] - NODES[m])
            w = suf[j] if pre[j] is None else (pre[j] if suf[j] is None else pre[j] * suf[j])
            w = w * c
            if ref is wz_ref:
                ref[:, j, :] = w
            else:
                ref[j] = w
    ids = turned[96:128, :].astype(i32)
    for copy in copies:
        copy.wait()
    parts = [split_two(u_ref[m]) for m in range(2)]
    cat = jnp.concatenate([parts[0][0], parts[1][0], parts[0][1], parts[1][1]], axis=1)
    rows = []
    for g in range(16):
        hot = [one_hot_rows(ids[s : s + 1, :], 256) for s in (2 * g, 2 * g + 1)]
        hot = jnp.concatenate(hot, axis=1)
        got = dot_nn(cat, jnp.concatenate([hot, hot], axis=0))
        for b in range(2):
            s = 2 * g + b
            total = None
            for j in range(8):
                acc = None
                for i in range(8):
                    term = wx_ref[i, s : s + 1, :] * got[i * 64 + j * 8 : i * 64 + j * 8 + 8, b * 128 : (b + 1) * 128]
                    acc = term if acc is None else acc + term
                acc = acc * wy_ref[j, s : s + 1, :]
                total = acc if total is None else total + acc
            rows.append(jnp.sum(total * wz_ref[s], axis=0, keepdims=True))
    answers = jnp.concatenate(rows, axis=0)
    blocks = [answers]
    for dx, dy in GHOSTS:
        blocks.append(pltpu.roll(answers, (-(4 * dx + dy)) % 128, 1))
    for a in range(3):
        group = blocks[4 * a : 4 * a + 4]
        if len(group) < 4:
            group = group + [jnp.zeros((32 * (4 - len(group)), 128), f32)]
        ans_ref[:, a, :] = jnp.concatenate(group, axis=0).T
    ans_ref[:, 3, :] = jnp.zeros((128, 128), f32)


def answer_kernel(u_ref, received_ref, ans_ref, wx_ref, wy_ref, wz_ref):
    interpolate(u_ref, received_ref, ans_ref, wx_ref, wy_ref, wz_ref, [])


def first_kernel(u_any, received_ref, ans_ref, u_ref, wx_ref, wy_ref, wz_ref, sems):
    copies = start_copies([(u_any, u_ref)], sems)
    interpolate(u_ref, received_ref, ans_ref, wx_ref, wy_ref, wz_ref, copies)


def edge_kernel(yl_ref, yr_ref, pair_ref, cross_ref, keep_ref, yl_out, yr_out):
    odd = keep_ref[2] > 0.5
    for m in range(2):
        for src, dst, j in ((yl_ref, yl_out, 0), (yr_ref, yr_out, 7)):
            mask = keep_ref[0 if j == 0 else 1]
            pair = pair_ref[m, j * 8 : j * 8 + 8, :]
            cross = cross_ref[m, j * 8 : j * 8 + 8, :]
            for i in range(8):
                val = src[m, i * 8 : i * 8 + 8, :]
                if i == 0:
                    val = val + jnp.where(odd, pair, cross)
                if i == 7:
                    val = val + jnp.where(odd, cross, pair)
                dst[m, i * 8 : i * 8 + 8, :] = val * mask


def bring_kernel(after_ref, table_any, ghost_any, received_any, table_ref, ghost_ref, received_ref, sems):
    copies = start_copies([(table_any, table_ref), (ghost_any, ghost_ref), (received_any, received_ref)], sems)
    for copy in copies:
        copy.wait()


def first_bring_kernel(after_ref, table_any, received_any, table_ref, received_ref, sems):
    copies = start_copies([(table_any, table_ref), (received_any, received_ref)], sems)
    for copy in copies:
        copy.wait()


def with_faces(parts, m, ij):
    loc_ref, pair_ref, cross_ref, yn_ref, yp_ref, keep_ref, ring = parts
    i, j = ij // 8, ij % 8
    val = loc_ref[m, ij * 8 : ij * 8 + 8, :]
    if j == 0:
        val = val + yp_ref[m, i * 8 : i * 8 + 8, :]
    elif j == 7:
        val = val + yn_ref[m, i * 8 : i * 8 + 8, :]
    if ring and i in (0, 7):
        val = val + (cross_ref if i == 0 else pair_ref)[m, j * 8 : j * 8 + 8, :]
    elif i in (0, 7):
        pair = pair_ref[m, j * 8 : j * 8 + 8, :]
        cross = cross_ref[m, j * 8 : j * 8 + 8, :]
        odd = keep_ref[2] > 0.5
        val = val + (jnp.where(odd, pair, cross) if i == 0 else jnp.where(odd, cross, pair))
    return val


def picked(block, owner, rank):
    parts = []
    for c in range(owner.shape[1] // 128):
        sl = slice(c * 128, (c + 1) * 128)
        index = jnp.broadcast_to(owner[:, sl], (32, 128))
        got = jnp.take_along_axis(block, index, axis=1, mode="promise_in_bounds")
        pick = lax.broadcasted_iota(i32, (32, 128), 0) == rank[:, sl]
        parts.append(jnp.sum(jnp.where(pick, got, 0.0), axis=0, keepdims=True))
    g = jnp.concatenate(parts, axis=1)
    return split_two(g)


def placed(row, count, hi, lo):
    at = lax.broadcasted_iota(jnp.int16, (count, row.shape[-1]), 0) == row.astype(jnp.int16)
    zero = jnp.zeros((), bf16)
    return jnp.concatenate([jnp.where(at, hi, zero), jnp.where(at, lo, zero)], axis=0)


def add_replies(replies_ref, table_ref, ghost_ref, parts, work_ref):
    half = table_ref.shape[1] // 2
    wk = weight_rows()
    blocks = []
    for a in range(3):
        turned = replies_ref[:, a, :].T
        for c in range(4):
            if 4 * a + c < 9:
                blocks.append(turned[c * 32 : c * 32 + 32, :])
    for m in range(2):
        sl = slice(m * half, (m + 1) * half)
        faces = {}
        for n, where in enumerate(GHOSTS):
            ghi, glo = picked(blocks[n + 1], ghost_ref[n, 0:1, sl], ghost_ref[n, 1:2, sl])
            size = 8 if where[0] and where[1] else 64
            lhs = placed(ghost_ref[n, 2:3, sl], size, ghi, glo)
            both = dot_nt(lhs, one_hot_rows(ghost_ref[n, 3:4, sl], 128))
            faces[where] = both[0:size, :] + both[size : 2 * size, :]
        ghi, glo = picked(blocks[0], table_ref[0:1, sl], table_ref[1:2, sl])
        point = table_ref[2:3, sl]
        q = lax.shift_right_logical(point, 7)
        e = lax.bitwise_and(point, 127)
        both = dot_nt(one_hot_rows(q, 512), placed(e, 128, ghi, glo))
        summed = both[:, 0:128] + both[:, 128:256]
        for ij in range(64):
            rows = slice(ij * 8, ij * 8 + 8)
            i, j = ij // 8, ij % 8
            dx = {0: -1, 7: 1}.get(i, 0)
            dy = {0: -1, 7: 1}.get(j, 0)
            c = penalty_rate * volume_factor * WEIGHTS[i] * WEIGHTS[j]
            g = summed[rows, :]
            if dx:
                g = g + faces[(dx, 0)][j * 8 : j * 8 + 8, :]
            if dy:
                g = g + faces[(0, dy)][i * 8 : i * 8 + 8, :]
            if dx and dy:
                g = g + faces[(dx, dy)]
            work_ref[m, rows, :] = with_faces(parts, m, ij) + (c * wk) * g


def advance(blend, start_ref, u_ref, inv_ref, work_ref, new_ref, meshes=(0, 1)):
    lane = lax.broadcasted_iota(i32, (64, 128), 1)
    for m in meshes:
        left = work_ref[m, pl.ds(0, 64, stride=8), :]
        right = work_ref[m, pl.ds(7, 64, stride=8), :]
        work_ref[m, pl.ds(0, 64, stride=8), :] = left + jnp.where(lane > 0, pltpu.roll(right, 1, 1), 0.0)
        work_ref[m, pl.ds(7, 64, stride=8), :] = right + jnp.where(lane < 127, pltpu.roll(left, 127, 1), 0.0)
        new = u_ref[m] + inv_ref[...] * work_ref[m]
        if blend is not None:
            new = blend[0] * start_ref[m] + blend[1] * new
        new_ref[m] = new


def step_kernel(blend, replies_ref, table_ref, ghost_ref, old_ref, xn_ref, xp_ref, yn_ref, yp_ref, kept_ref, start_any, u_any, inv_any, vel_any, nu_any, load_any,
                deep_any, mask_any, new_any, new_ref, loc_ref, xl_ref, xr_ref, yl_ref, yr_ref, keep_ref,
                work_ref, start_ref, u_ref, inv_ref, vel_ref, nu_ref, load_ref, deep_ref, mask_ref,
                ax_ref, ay_ref, fz_ref, sems):
    copies = start_copies(
        [(u_any, u_ref), (inv_any, inv_ref), (start_any, start_ref), (deep_any, deep_ref), (nu_any, nu_ref),
         (vel_any, vel_ref), (load_any, load_ref), (mask_any, mask_ref)],
        sems,
    )
    add_replies(replies_ref, table_ref, ghost_ref, (old_ref, xn_ref, xp_ref, yn_ref, yp_ref, kept_ref, blend is None), work_ref)
    for copy in copies[:4]:
        copy.wait()
    advance(blend, start_ref, u_ref, inv_ref, work_ref, new_ref)
    out = pltpu.make_async_copy(new_ref, new_any, sems.at[8])
    out.start()
    local_rates(new_ref, vel_ref, nu_ref, load_ref, deep_ref, loc_ref, ax_ref, ay_ref, fz_ref, copies[4:])
    send_faces(loc_ref, mask_ref, xl_ref, xr_ref, yl_ref, yr_ref, keep_ref)
    out.wait()


def last_kernel(blend, replies_ref, table_ref, ghost_ref, old_ref, xn_ref, xp_ref, yn_ref, yp_ref, kept_ref, start_any, u_any, inv_any, new_any,
                work_ref, start_ref, u_ref, inv_ref, new_ref, sems):
    copies = start_copies([(u_any, u_ref), (inv_any, inv_ref), (start_any, start_ref)], sems)
    add_replies(replies_ref, table_ref, ghost_ref, (old_ref, xn_ref, xp_ref, yn_ref, yp_ref, kept_ref, blend is None), work_ref)
    for copy in copies:
        copy.wait()
    outs = []
    for m in range(2):
        advance(blend, start_ref, u_ref, inv_ref, work_ref, new_ref, (m,))
        outs.append(pltpu.make_async_copy(new_ref.at[m], new_any.at[m], sems.at[3 + m]))
        outs[m].start()
    for out in outs:
        out.wait()


PINNED = "ap"
SPACES = {"p": pltpu.VMEM, "v": pltpu.VMEM, "a": pltpu.HBM, "s": pltpu.SMEM}


def call(kernel, outs, ins, scratch=(), spaces="", out_spaces=""):
    return pl.pallas_call(
        kernel,
        out_shape=[SPACES[c](s, d) if c in PINNED else jax.ShapeDtypeStruct(s, d) for (s, d), c in zip(outs, out_spaces)],
        in_specs=[pl.BlockSpec(memory_space=SPACES[c]) for c in spaces],
        out_specs=[pl.BlockSpec(memory_space=SPACES[c]) for c in out_spaces],
        scratch_shapes=list(scratch),
        compiler_params=pltpu.CompilerParams(vmem_limit_bytes=28 << 20),
    )(*[pltpu.with_memory_space_constraint(x, SPACES[c]) if c in PINNED else x for x, c in zip(ins, spaces)])


def passed_around(value, axis, steps):
    count = lax.axis_size(axis)
    return lax.ppermute(value, axis, [(n, (n + steps) % count) for n in range(count)])


def swapped(pair, cross):
    count = lax.axis_size("gx")
    across = [min(max(((n + 1) ^ 1) - 1, 0), count - 1) for n in range(count)]
    return (
        lax.ppermute(pair, "gx", [(n, n ^ 1) for n in range(count)]),
        lax.ppermute(cross, "gx", [(n, across[n]) for n in range(count)]),
    )


def exchange(x):
    return lax.all_to_all(x, ("gx", "gy"), split_axis=0, concat_axis=0, tiled=True)


def body(scalar, velocity, diffusivity, recv_owner, donor_elem, recv_point, recv_coords):
    rows = recv_owner.shape[0]
    field = (2, 512, 128)
    face = (2, 64, 128)
    start = scalar.reshape(field)
    flow = velocity.reshape((3,) + field)
    nu = diffusivity.reshape(2, 128)
    owner = recv_owner.reshape(1, rows)
    donor = donor_elem.reshape(1, rows)
    point = recv_point.reshape(1, rows)
    deep = jnp.asarray(np.stack([block_matrix(DERIV), block_matrix(DERIV_T)]))

    def vmem(shape, dtype=f32):
        return pltpu.VMEM(shape, dtype)

    def dma(count):
        return pltpu.SemaphoreType.DMA((count,))

    line = vmem((1, rows), i32)
    weights_scratch = [vmem((8, 32, 128)), vmem((8, 32, 128)), vmem((32, 8, 128))]
    local_scratch = [vmem((3,) + field), vmem((2, 128)), vmem(field), vmem((2, 128, 384), bf16), vmem((5, 8, 128))]
    local_scratch = local_scratch + [vmem(field)] * 3
    tables = [((3, rows), i32)] * 2

    payload, rank = call(
        query_kernel,
        [((128, 128), f32), ((1, rows), i32)],
        (owner, donor, recv_coords),
        [line, line, vmem((3, rows)), line, dma(4)],
        "aaa",
        "va",
    )
    received = exchange(payload)

    ix, iy = lax.axis_index("gx"), lax.axis_index("gy")
    inside = [ix > 0, ix < lax.axis_size("gx") - 1, iy > 0, iy < lax.axis_size("gy") - 1]
    flags = jnp.stack(inside + [ix % 2 == 1]).astype(i32)
    load, inv, table, mask, low, high = call(
        prepare_kernel,
        [(field, f32), ((512, 128), f32), ((3, rows), i32), ((5, 8, 128), f32)] + tables,
        (flags, owner, rank, point),
        [vmem(field), vmem((512, 128)), vmem((3, rows), i32), vmem((5, 8, 128))]
        + [vmem((3, rows), i32)] * 2
        + [dma(6)],
        "saaa",
        "aaaaaa",
    )

    def along_y(yl, yr):
        return passed_around(yl, "gy", -1), passed_around(yr, "gy", 1)

    def faces_along_y(yl, yr, xn, xp, keep):
        return along_y(*call(edge_kernel, [(face, f32)] * 2, (yl, yr, xn, xp, keep), (), "vvvvv", "vv"))

    def bring(after):
        return call(
            bring_kernel,
            [((3, rows), i32), ((8, 4, rows), i32), ((128, 128), f32)],
            (after, table, ghosts, received),
            [dma(3)],
            "vaaa",
            "vvv",
        )

    outs = [(field, f32)] + [(face, f32)] * 4 + [((3, 8, 128), f32)]
    u = start
    loc, xl, xr, yl, yr, keep = call(
        local_kernel,
        outs,
        (u, flow, nu, load, deep, mask),
        [vmem(field)] + local_scratch + [dma(6)],
        "aaaaaa",
        "vvvvvv",
    )
    received, loc, yl, yr, low, high = lax.optimization_barrier((received, loc, yl, yr, low, high))
    yn, yp = along_y(yl, yr)
    table_n, table_p = along_y(low, high)
    answers = call(
        first_kernel,
        [((128, 4, 128), f32)],
        (u, received),
        [vmem(field)] + weights_scratch + [dma(1)],
        "av",
        "p",
    )[0]
    answers, yn, yp, table_n, table_p = lax.optimization_barrier((answers, yn, yp, table_n, table_p))
    replies = exchange(answers)
    xl, xr = call(first_edge_kernel, [(face, f32)] * 2, (xl, xr, yn, yp, keep), (), "vvvvv", "vv")
    xn, xp = passed_around(xl, "gx", -1), passed_around(xr, "gx", 1)
    low, high = call(
        relay_kernel, [((9, rows), i32)] * 2, (flags, table, table_p, table_n), (), "svvv", "vv"
    )
    tables_n, tables_p = passed_around(low, "gx", -1), passed_around(high, "gx", 1)
    near, ghosts = call(
        ghost_kernel,
        [((8, 4, rows), i32)] * 2,
        (tables_p, tables_n, table_p, table_n),
        [dma(1)],
        "vvvv",
        "va",
    )
    own, asked = call(
        first_bring_kernel,
        [((3, rows), i32), ((128, 128), f32)],
        (table_n, table, received),
        [dma(2)],
        "vaa",
        "vv",
    )
    for blend in (None, (0.75, 0.25)):
        u, near_u, loc, xl, xr, yl, yr, keep = call(
            lambda *refs, blend=blend: step_kernel(blend, *refs),
            [(field, f32)] * 2 + outs,
            (replies, own, near, loc, xn, xp, yn, yp, keep, start, u, inv, flow, nu, load, deep, mask),
            [vmem(field)] * 3 + [vmem((512, 128))] + local_scratch + [dma(9)],
            "vvvvvvvvvaaaaaaaa",
            "avvvvvvv",
        )
        xn, xp = swapped(xl, xr)
        answers = call(
            answer_kernel,
            [((128, 4, 128), f32)],
            (near_u, asked),
            weights_scratch,
            "vv",
            "p",
        )[0]
        answers, xn, xp = lax.optimization_barrier((answers, xn, xp))
        replies = exchange(answers)
        yn, yp = faces_along_y(yl, yr, xn, xp, keep)
        own, near, asked = bring(keep)
    third = call(
        lambda *refs: last_kernel((1.0 / 3.0, 2.0 / 3.0), *refs),
        [(field, f32)],
        (replies, own, near, loc, xn, xp, yn, yp, keep, start, u, inv),
        [vmem(field)] * 3 + [vmem((512, 128)), vmem(field), dma(5)],
        "vvvvvvvvvaaa",
        "a",
    )[0]
    return third.reshape(scalar.shape)


def solution(mesh):
    return jax.shard_map(
        body,
        mesh=mesh,
        in_specs=(
            P(None, None, "gx", "gy", None),
            P(None, None, None, "gx", "gy", None),
            P(None, "gx", "gy", None),
            P(("gx", "gy"), None),
            P(("gx", "gy")),
            P(("gx", "gy")),
            P(None, ("gx", "gy")),
        ),
        out_specs=P(None, None, "gx", "gy", None),
        check_vma=False,
    )
```
